128 devices in a mesh: fsdp: 16 (over z, y), tensor: 8 (over x, core).
Axes of the slice: x: 4, y: 4, z: 4, core: 2. Of those that a mesh axis runs over, the one named last changes fastest.
Arguments:
- grad_blocks: bfloat16 [2, 16896, 1536], P(None, 'tensor', 'fsdp'), may hold values from -150 to 150
- master_shard: float32 [2, 16896, 1536], P(None, ('fsdp', 'tensor')), may hold values from -6 to 6
- first_moment: float32 [2, 16896, 1536], P(None, ('fsdp', 'tensor')), may hold values from -2 to 2
- second_moment: float32 [2, 16896, 1536], P(None, ('fsdp', 'tensor')), may hold values from 0.05 to 0.5
- average_shard: float32 [2, 16896, 1536], P(None, ('tensor', 'fsdp')), may hold values from -6 to 6
- gain_grads: bfloat16 [2, 3072], P(None, ('fsdp', 'tensor')), may hold values from -24 to 24
- gain_master: float32 [2, 3072], P(None, ('fsdp', 'tensor')), may hold values from 0.5 to 1.5
- gain_first: float32 [2, 3072], P(None, ('fsdp', 'tensor')), may hold values from -2 to 2
- gain_second: float32 [2, 3072], P(None, ('fsdp', 'tensor')), may hold values from 0.05 to 0.5
- gain_average: float32 [2, 3072], P(None, ('fsdp', 'tensor')), may hold values from 0.5 to 1.5
Outputs:
- train_weights: bfloat16 [2, 16896, 1536], P(None, 'tensor', 'fsdp')
- master_next: float32 [2, 16896, 1536], P(None, ('fsdp', 'tensor'))
- first_next: float32 [2, 16896, 1536], P(None, ('fsdp', 'tensor'))
- second_next: float32 [2, 16896, 1536], P(None, ('fsdp', 'tensor'))
- average_next: float32 [2, 16896, 1536], P(None, ('tensor', 'fsdp'))
- gain_weights: bfloat16 [2, 3072], replicated
- master_gains: float32 [2, 3072], P(None, ('fsdp', 'tensor'))
- first_gains: float32 [2, 3072], P(None, ('fsdp', 'tensor'))
- second_gains: float32 [2, 3072], P(None, ('fsdp', 'tensor'))
- average_gains: float32 [2, 3072], P(None, ('fsdp', 'tensor'))
The draws below stay inside these ranges and needn't reach their ends.
All inputs are finite; a program needn't handle non-finite values.
Results may differ from the reference program's by a relative error of at most 0.001.
Values may be sent and summed in bfloat16 or wider, within the bound.
A program may use at most 128 MiB of HBM per device.

```python
import math
import jax
import jax.numpy as jnp

D = 1536
LAYERS = 2
STEP = 20
COLS = 16896


def draw_grad_blocks(key, part):
    row_key, col_key, value_key = jax.random.split(key, 3)
    row_ramp = jnp.arange(COLS, dtype=jnp.float32) / COLS
    row_scale = jnp.exp(jnp.log(3.0) * row_ramp + jax.random.uniform(row_key, (COLS,), jnp.float32, 0.0, jnp.log(4.0)))
    col_scale = jnp.exp(jax.random.uniform(col_key, (D,), jnp.float32, 0.0, jnp.log(3.0)))
    basic_draw = jnp.clip(jax.random.normal(value_key, (LAYERS, COLS, D), jnp.float32), -4.0, 4.0)
    values = basic_draw * row_scale[None, :, None] * col_scale[None, None, :]
    return values.astype(jnp.bfloat16)


def block_levels(key, shape, shards, low, largest):
    def one(dim, shards_of):
        steps = jax.random.uniform(jax.random.fold_in(jax.random.fold_in(key, 6), dim), (shards_of,), jnp.float32, low / len(shards), largest / len(shards))
        return jnp.repeat(jnp.exp(steps), shape[dim] // shards_of).reshape((-1,) + (1,) * (len(shape) - dim - 1))

    gain = one(*shards[0])
    for cut in shards[1:]:
        gain = gain * one(*cut)
    return gain


def gaussian(rng, shape, deviation, most, shards=(), kind=jnp.bfloat16):
    values = jax.random.normal(rng, shape, jnp.float32) * deviation
    if len(shards) > 0:
        values = block_levels(rng, shape, shards, -0.22, 0.18) * values
    return jnp.clip(values, min=-most, max=most).astype(kind)


def setup_inputs(seed: int = 0) -> dict:
    key_of = jax.random.split(jax.random.key(seed), 11)
    grad_blocks = draw_grad_blocks(jax.random.fold_in(key_of[10], 71), 0)
    master_shard = gaussian(key_of[1], (LAYERS, COLS, D), 1.0, 6.0, ((1, 128),), jnp.float32)
    first_moment = gaussian(key_of[2], (LAYERS, COLS, D), 0.3, 2.0, ((1, 128),), jnp.float32)
    second_moment = jnp.clip(jnp.exp(math.log(0.5) - 2.3025851 * jax.random.uniform(key_of[3], (LAYERS, COLS, D), jnp.float32) ** block_levels(key_of[3], (LAYERS, COLS, D), ((1, 128),), -0.2, 0.2)), 0.05, 0.5)
    average_shard = gaussian(key_of[4], (LAYERS, COLS, D), 1.0, 6.0, ((1, 128),), jnp.float32)
    gain_grads = gaussian(key_of[5], (LAYERS, 2 * D), 6.0, 24.0, ((1, 128),))
    gain_master = jnp.clip(1.0 + 0.1 * jax.random.normal(key_of[6], (LAYERS, 2 * D), jnp.float32), 0.5, 1.5)
    gain_first = gaussian(key_of[7], (LAYERS, 2 * D), 0.3, 2.0, ((1, 128),), jnp.float32)
    gain_second = jnp.clip(jnp.exp(math.log(0.5) - 2.3025851 * jax.random.uniform(key_of[8], (LAYERS, 2 * D), jnp.float32) ** block_levels(key_of[8], (LAYERS, 2 * D), ((1, 128),), -0.2, 0.2)), 0.05, 0.5)
    gain_average = jnp.clip(1.0 + 0.1 * jax.random.normal(key_of[9], (LAYERS, 2 * D), jnp.float32), 0.5, 1.5)
    return {"grad_blocks": grad_blocks, "master_shard": master_shard, "first_moment": first_moment, "second_moment": second_moment, "average_shard": average_shard, "gain_grads": gain_grads, "gain_master": gain_master, "gain_first": gain_first, "gain_second": gain_second, "gain_average": gain_average}


learn_rate = 0.1
weight_decay = 0.1
beta_first = 0.9
beta_second = 0.95
adam_epsilon = 1e-08
average_decay = 0.9
clip_level = 0.5
mean_epsilon = 1e-06

def adam_step(gradient, master, first_state, second_state, clip_scale):
    clipped = gradient.astype(jnp.float32) * clip_scale
    first_new = beta_first * first_state + (1.0 - beta_first) * clipped
    second_new = beta_second * second_state + (1.0 - beta_second) * clipped * clipped
    first_fix = 1.0 - beta_first ** STEP
    second_fix = 1.0 - beta_second ** STEP
    direction = first_new / first_fix / (jnp.sqrt(second_new / second_fix) + adam_epsilon) + weight_decay * master
    master_new = master - learn_rate * direction
    return (master_new, first_new, second_new)

def reference(grad_blocks, master_shard, first_moment, second_moment, average_shard, gain_grads, gain_master, gain_first, gain_second, gain_average):
    widened = grad_blocks.astype(jnp.float32)
    gain_wide = gain_grads.astype(jnp.float32)
    squares = jnp.sum(widened * widened) + jnp.sum(gain_wide * gain_wide)
    entries = LAYERS * (COLS * D + 2 * D)
    clip_scale = jnp.minimum(1.0, clip_level / jnp.sqrt(squares / entries + mean_epsilon))
    master_next, first_next, second_next = adam_step(grad_blocks, master_shard, first_moment, second_moment, clip_scale)
    average_next = average_decay * average_shard + (1.0 - average_decay) * master_next
    master_gains, first_gains, second_gains = adam_step(gain_grads, gain_master, gain_first, gain_second, clip_scale)
    average_gains = average_decay * gain_average + (1.0 - average_decay) * master_gains
    return (master_next.astype(jnp.bfloat16), master_next, first_next, second_next, average_next, master_gains.astype(jnp.bfloat16), master_gains, first_gains, second_gains, average_gains)
```

```python
import jax
import jax.numpy as jnp
from jax import lax
from jax.experimental import pallas as pl
from jax.experimental.pallas import tpu as pltpu
from jax.sharding import PartitionSpec as P

STEP = 20


learn_rate = 0.1
weight_decay = 0.1
beta_first = 0.9
beta_second = 0.95
adam_epsilon = 1e-08
average_decay = 0.9
clip_level = 0.5
mean_epsilon = 1e-06

MESH = pl.DeviceIdType.MESH
FSDP = 16
TENSOR = 8


def adam_step(gradient, master, first_state, second_state, clip_scale):
    clipped = gradient.astype(jnp.float32) * clip_scale
    first_new = beta_first * first_state + (1.0 - beta_first) * clipped
    second_new = beta_second * second_state + (1.0 - beta_second) * clipped * clipped
    first_fix = 1.0 - beta_first**STEP
    second_fix = 1.0 - beta_second**STEP
    direction = (
        first_new / first_fix / (jnp.sqrt(second_new / second_fix) + adam_epsilon)
        + weight_decay * master
    )
    master_new = master - learn_rate * direction
    return (master_new, first_new, second_new)


def enter(f, t):
    barrier = pltpu.get_barrier_semaphore()

    @pl.loop(1, TENSOR)
    def _(i):
        pl.semaphore_signal(
            barrier, inc=1, device_id=(f, lax.rem(t + i, TENSOR)), device_id_type=MESH
        )

    @pl.loop(1, FSDP)
    def _(i):
        pl.semaphore_signal(
            barrier, inc=1, device_id=(lax.rem(f + i, FSDP), t), device_id_type=MESH
        )

    pl.semaphore_wait(barrier, TENSOR + FSDP - 2)


def remote(source, target, send_sem, recv_sem, device):
    return pltpu.make_async_remote_copy(
        src_ref=source,
        dst_ref=target,
        send_sem=send_sem,
        recv_sem=recv_sem,
        device_id=device,
        device_id_type=MESH,
    )


def send(source, target, send_sem, recv_sem, device, is_own):
    @pl.when(is_own)
    def _():
        pltpu.make_async_copy(source, target, recv_sem).start()

    @pl.when(jnp.logical_not(is_own))
    def _():
        remote(source, target, send_sem, recv_sem, device).start()


def sent(source, target, send_sem, recv_sem, device, is_own):
    @pl.when(jnp.logical_not(is_own))
    def _():
        remote(source, target, send_sem, recv_sem, device).wait_send()


def arrived(target, recv_sem):
    pltpu.make_async_copy(target, target, recv_sem).wait()


def small_copies(f, t, small_ref, all_ref, sems):
    row_send, row_recv, col_send, col_recv = sems

    def row_copy(i):
        return remote(
            small_ref,
            all_ref.at[f, t],
            row_send.at[i],
            row_recv.at[t],
            (f, lax.rem(t + i, TENSOR)),
        )

    def col_copy(i):
        return remote(
            all_ref.at[f],
            all_ref.at[f],
            col_send.at[i],
            col_recv.at[f],
            (lax.rem(f + i, FSDP), t),
        )

    return row_copy, col_copy


def small_first(f, t, small_ref, all_ref, sems):
    row_copy, _ = small_copies(f, t, small_ref, all_ref, sems)
    pltpu.make_async_copy(small_ref, all_ref.at[f, t], sems[1].at[t]).start()

    @pl.loop(1, TENSOR)
    def _(i):
        row_copy(i).start()


def small_second(f, t, small_ref, all_ref, sems):
    _, col_copy = small_copies(f, t, small_ref, all_ref, sems)

    @pl.loop(0, TENSOR)
    def _(i):
        arrived(all_ref.at[f, i], sems[1].at[i])

    @pl.loop(1, FSDP)
    def _(i):
        col_copy(i).start()


def small_done(f, t, small_ref, all_ref, sems):
    row_copy, col_copy = small_copies(f, t, small_ref, all_ref, sems)

    @pl.loop(1, FSDP)
    def _(i):
        source = lax.rem(f + i, FSDP)
        arrived(all_ref.at[source], sems[3].at[source])

    @pl.loop(1, TENSOR)
    def _(i):
        row_copy(i).wait_send()

    @pl.loop(1, FSDP)
    def _(i):
        col_copy(i).wait_send()


def gather_kernel(
    wire, small, out, sums, mid, send_a, recv_a, send_b, recv_b, rs, rr, cs, cr
):
    f = lax.axis_index("fsdp")
    t = lax.axis_index("tensor")
    sems = (rs, rr, cs, cr)
    enter(f, t)
    small_first(f, t, small, sums, sems)
    small_second(f, t, small, sums, sems)

    def stage_a(n):
        i, half = n // 2, lax.rem(n + f // TENSOR, 2)
        to = lax.rem(t + i + f, TENSOR)
        k = half * TENSOR + to
        slot = 2 * t + half
        return (
            wire.at[k], mid.at[slot], send_a.at[k], recv_a.at[slot], (f, to), to == t,
        )

    def stage_b(n):
        i, half = n // 2, lax.rem(n + f // TENSOR, 2)
        m = 2 * lax.rem(t - i - f + 4 * TENSOR, TENSOR) + half
        return m, (mid.at[m], out.at[f], send_b.at[m], recv_b.at[f], (m, t), m == f)

    @pl.loop(0, FSDP)
    def _(n):
        send(*stage_a(n))

    @pl.loop(0, FSDP)
    def _(n):
        m, copy = stage_b(n)
        arrived(mid.at[m], recv_a.at[m])
        send(*copy)

    @pl.loop(0, FSDP)
    def _(n):
        arrived(out.at[n], recv_b.at[n])

    small_done(f, t, small, sums, sems)

    @pl.loop(0, FSDP)
    def _(n):
        sent(*stage_a(n))
        sent(*stage_b(n)[1])


def spread_kernel(
    wire, small, train, average, gains, mid,
    send_a, recv_a, send_b, recv_b, send_c, recv_c, rs, rr, cs, cr,
):
    f = lax.axis_index("fsdp")
    t = lax.axis_index("tensor")
    sems = (rs, rr, cs, cr)
    enter(f, t)
    small_first(f, t, small, gains, sems)

    def stage_a(n):
        j = lax.rem(f + n + 2 * t, FSDP)
        return (wire.at[j], mid.at[f], send_a.at[j], recv_a.at[f], (j, t), j == f)

    def stage_b(n):
        source = lax.rem(f - n - 2 * t + 2 * FSDP, FSDP)
        to = source // 2
        k = lax.rem(source, 2) * TENSOR + t
        return source, (
            mid.at[source], train.at[k], send_b.at[source], recv_b.at[k], (f, to), to == t,
        )

    def stage_c(n):
        k = lax.rem(n, 2) * TENSOR + lax.rem(n // 2 + f + t, TENSOR)
        return k, (train.at[k], average.at[f], send_c.at[k], recv_c.at[f], (k, t), k == f)

    @pl.loop(0, FSDP)
    def _(n):
        send(*stage_a(n))

    @pl.loop(0, FSDP)
    def _(n):
        source, copy = stage_b(n)
        arrived(mid.at[source], recv_a.at[source])
        send(*copy)

    small_second(f, t, small, gains, sems)

    @pl.loop(0, FSDP)
    def _(n):
        k, copy = stage_c(n)
        arrived(train.at[k], recv_b.at[k])
        send(*copy)

    @pl.loop(0, FSDP)
    def _(n):
        arrived(average.at[n], recv_c.at[n])

    small_done(f, t, small, gains, sems)

    @pl.loop(0, FSDP)
    def _(n):
        sent(*stage_a(n))
        sent(*stage_b(n)[1])
        sent(*stage_c(n)[1])


def exchange(kernel, wire, small, outputs, stages, collective_id):
    vmem = pl.BlockSpec(memory_space=pltpu.VMEM)
    pieces = jax.ShapeDtypeStruct(wire.shape, wire.dtype)
    dma = pltpu.SemaphoreType.DMA
    return pl.pallas_call(
        kernel,
        out_shape=[pieces] * outputs
        + [jax.ShapeDtypeStruct((FSDP, TENSOR) + small.shape, small.dtype)],
        in_specs=[vmem] * 2,
        out_specs=[vmem] * (outputs + 1),
        scratch_shapes=[pltpu.VMEM(wire.shape, wire.dtype)]
        + [dma((FSDP,))] * (2 * stages)
        + [dma((TENSOR,)), dma((TENSOR,)), dma((FSDP,)), dma((FSDP,))],
        compiler_params=pltpu.CompilerParams(
            collective_id=collective_id, has_side_effects=True
        ),
    )(wire, small)


def on_device(
    grad_blocks,
    master_shard,
    first_moment,
    second_moment,
    average_shard,
    gain_grads,
    gain_master,
    gain_first,
    gain_second,
    gain_average,
):
    layers, block_rows, block_cols = grad_blocks.shape
    rows = block_rows // FSDP
    width = block_cols * FSDP
    entries = (grad_blocks.size + gain_grads.size) * FSDP * TENSOR

    wide = grad_blocks.astype(jnp.float32)
    gain_wide = gain_grads.astype(jnp.float32)
    squares = jnp.sum(wide * wide) + jnp.sum(gain_wide * gain_wide)
    small = jnp.pad(squares.reshape(1, 1), ((0, 0), (0, 127)))
    wire = grad_blocks.reshape(layers, FSDP, rows, block_cols).transpose(1, 0, 2, 3)
    pieces, sums = exchange(gather_kernel, wire, small, 1, 2, 0)
    total_squares = jnp.sum(sums)
    clip_scale = jnp.minimum(1.0, clip_level / jnp.sqrt(total_squares / entries + mean_epsilon))

    def turned(x):
        return x.transpose(1, 0, 2)

    grads = pieces.transpose(2, 1, 0, 3).reshape(rows, layers, width)
    master_next, first_next, second_next = adam_step(
        grads, turned(master_shard), turned(first_moment), turned(second_moment), clip_scale
    )
    master_gains, first_gains, second_gains = adam_step(
        gain_grads, gain_master, gain_first, gain_second, clip_scale
    )
    average_gains = average_decay * gain_average + (1.0 - average_decay) * master_gains

    gain_count = gain_grads.size
    gain_cols = gain_grads.shape[1]
    gain_small = jnp.pad(
        master_gains.astype(jnp.bfloat16).astype(jnp.float32).reshape(1, gain_count),
        ((0, 0), (0, 128 - gain_count)),
    )
    out_wire = (
        master_next.astype(jnp.bfloat16)
        .reshape(rows, layers, FSDP, block_cols)
        .transpose(2, 1, 0, 3)
    )
    train, averages, gains = exchange(spread_kernel, out_wire, gain_small, 2, 3, 1)
    train_weights = train.transpose(1, 0, 2, 3).reshape(layers, block_rows, block_cols)
    layout = averages.transpose(2, 1, 0, 3).reshape(rows, layers, width).astype(jnp.float32)
    average_next = average_decay * turned(average_shard) + (1.0 - average_decay) * layout
    gain_weights = (
        gains.reshape(FSDP * TENSOR, 128)[:, :gain_count]
        .reshape(FSDP * TENSOR, layers, gain_cols)
        .transpose(1, 0, 2)
        .reshape(layers, FSDP * TENSOR * gain_cols)
        .astype(jnp.bfloat16)
    )
    return (
        train_weights,
        turned(master_next),
        turned(first_next),
        turned(second_next),
        turned(average_next),
        gain_weights,
        master_gains,
        first_gains,
        second_gains,
        average_gains,
    )


def solution(mesh):
    flat = P(None, ("fsdp", "tensor"), None)
    gain = P(None, ("fsdp", "tensor"))
    blocks = P(None, "tensor", "fsdp")
    averaging = P(None, ("tensor", "fsdp"), None)
    return jax.shard_map(
        on_device,
        mesh=mesh,
        in_specs=(blocks, flat, flat, flat, averaging, gain, gain, gain, gain, gain),
        out_specs=(blocks, flat, flat, flat, averaging, P(), gain, gain, gain, gain),
        check_vma=False,
    )
```

```python
import jax
import jax.numpy as jnp
from jax import lax
from jax.experimental import pallas as pl
from jax.experimental.pallas import tpu as pltpu
from jax.sharding import PartitionSpec as P

STEP = 20


learn_rate = 0.1
weight_decay = 0.1
beta_first = 0.9
beta_second = 0.95
adam_epsilon = 1e-08
average_decay = 0.9
clip_level = 0.5
mean_epsilon = 1e-06

MESH = pl.DeviceIdType.MESH
FSDP = 16
TENSOR = 8
SPAN = 384


def adam_step(gradient, master, first_state, second_state, clip_scale):
    clipped = gradient.astype(jnp.float32) * clip_scale
    first_new = beta_first * first_state + (1.0 - beta_first) * clipped
    second_new = beta_second * second_state + (1.0 - beta_second) * clipped * clipped
    first_fix = 1.0 - beta_first**STEP
    second_fix = 1.0 - beta_second**STEP
    direction = (
        first_new / first_fix / (jnp.sqrt(second_new / second_fix) + adam_epsilon)
        + weight_decay * master
    )
    master_new = master - learn_rate * direction
    return (master_new, first_new, second_new)


def enter(f, t):
    barrier = pltpu.get_barrier_semaphore()

    @pl.loop(1, TENSOR)
    def _(i):
        pl.semaphore_signal(
            barrier, inc=1, device_id=(f, lax.rem(t + i, TENSOR)), device_id_type=MESH
        )

    @pl.loop(1, FSDP)
    def _(i):
        pl.semaphore_signal(
            barrier, inc=1, device_id=(lax.rem(f + i, FSDP), t), device_id_type=MESH
        )

    pl.semaphore_wait(barrier, TENSOR + FSDP - 2)


def remote(source, target, send_sem, recv_sem, device):
    return pltpu.make_async_remote_copy(
        src_ref=source,
        dst_ref=target,
        send_sem=send_sem,
        recv_sem=recv_sem,
        device_id=device,
        device_id_type=MESH,
    )


def send(source, target, send_sem, recv_sem, device, is_own):
    @pl.when(is_own)
    def _():
        pltpu.make_async_copy(source, target, recv_sem).start()

    @pl.when(jnp.logical_not(is_own))
    def _():
        remote(source, target, send_sem, recv_sem, device).start()


def sent(source, target, send_sem, recv_sem, device, is_own):
    @pl.when(jnp.logical_not(is_own))
    def _():
        remote(source, target, send_sem, recv_sem, device).wait_send()


def arrived(target, recv_sem):
    pltpu.make_async_copy(target, target, recv_sem).wait()


def small_copies(f, t, small_ref, all_ref, sems):
    row_send, row_recv, col_send, col_recv = sems

    def row_copy(i):
        return remote(
            small_ref,
            all_ref.at[f, t],
            row_send.at[i],
            row_recv.at[t],
            (f, lax.rem(t + i, TENSOR)),
        )

    def col_copy(i):
        return remote(
            all_ref.at[f],
            all_ref.at[f],
            col_send.at[i],
            col_recv.at[f],
            (lax.rem(f + i, FSDP), t),
        )

    return row_copy, col_copy


def small_first(f, t, small_ref, all_ref, sems):
    row_copy, _ = small_copies(f, t, small_ref, all_ref, sems)
    pltpu.make_async_copy(small_ref, all_ref.at[f, t], sems[1].at[t]).start()

    @pl.loop(1, TENSOR)
    def _(i):
        row_copy(i).start()


def small_second(f, t, small_ref, all_ref, sems):
    _, col_copy = small_copies(f, t, small_ref, all_ref, sems)

    @pl.loop(0, TENSOR)
    def _(i):
        arrived(all_ref.at[f, i], sems[1].at[i])

    @pl.loop(1, FSDP)
    def _(i):
        col_copy(i).start()


def small_done(f, t, small_ref, all_ref, sems):
    row_copy, col_copy = small_copies(f, t, small_ref, all_ref, sems)

    @pl.loop(1, FSDP)
    def _(i):
        source = lax.rem(f + i, FSDP)
        arrived(all_ref.at[source], sems[3].at[source])

    @pl.loop(1, TENSOR)
    def _(i):
        row_copy(i).wait_send()

    @pl.loop(1, FSDP)
    def _(i):
        col_copy(i).wait_send()


def gather_kernel(
    wire, small, out, sums, mid, send_a, recv_a, send_b, recv_b, rs, rr, cs, cr
):
    f = lax.axis_index("fsdp")
    t = lax.axis_index("tensor")
    sems = (rs, rr, cs, cr)
    enter(f, t)
    small_first(f, t, small, sums, sems)
    small_second(f, t, small, sums, sems)

    def stage_a(n):
        i, half = n // 2, lax.rem(n + f // TENSOR, 2)
        to = lax.rem(t + i + f, TENSOR)
        k = half * TENSOR + to
        slot = 2 * t + half
        return (
            wire.at[k], mid.at[slot], send_a.at[k], recv_a.at[slot], (f, to), to == t,
        )

    def stage_b(n):
        i, half = n // 2, lax.rem(n + f // TENSOR, 2)
        m = 2 * lax.rem(t - i - f + 4 * TENSOR, TENSOR) + half
        return m, (mid.at[m], out.at[f], send_b.at[m], recv_b.at[f], (m, t), m == f)

    @pl.loop(0, FSDP)
    def _(n):
        send(*stage_a(n))

    @pl.loop(0, FSDP)
    def _(n):
        m, copy = stage_b(n)
        arrived(mid.at[m], recv_a.at[m])
        send(*copy)

    @pl.loop(0, FSDP)
    def _(n):
        arrived(out.at[n], recv_b.at[n])

    small_done(f, t, small, sums, sems)

    @pl.loop(0, FSDP)
    def _(n):
        sent(*stage_a(n))
        sent(*stage_b(n)[1])


def spread_kernel(
    wire, small, train, average, gains, mid,
    send_a, recv_a, send_b, recv_b, send_c, recv_c, rs, rr, cs, cr,
):
    f = lax.axis_index("fsdp")
    t = lax.axis_index("tensor")
    sems = (rs, rr, cs, cr)
    enter(f, t)
    small_first(f, t, small, gains, sems)

    def stage_a(n):
        j = lax.rem(f + n + 2 * t, FSDP)
        return (wire.at[j], mid.at[f], send_a.at[j], recv_a.at[f], (j, t), j == f)

    def stage_b(n):
        source = lax.rem(f - n - 2 * t + 2 * FSDP, FSDP)
        to = source // 2
        k = lax.rem(source, 2) * TENSOR + t
        return source, (
            mid.at[source], train.at[k], send_b.at[source], recv_b.at[k], (f, to), to == t,
        )

    def stage_c(n):
        k = lax.rem(n, 2) * TENSOR + lax.rem(n // 2 + f + t, TENSOR)
        return k, (train.at[k], average.at[f], send_c.at[k], recv_c.at[f], (k, t), k == f)

    @pl.loop(0, FSDP)
    def _(n):
        send(*stage_a(n))

    @pl.loop(0, FSDP)
    def _(n):
        source, copy = stage_b(n)
        arrived(mid.at[source], recv_a.at[source])
        send(*copy)

    small_second(f, t, small, gains, sems)

    @pl.loop(0, FSDP)
    def _(n):
        k, copy = stage_c(n)
        arrived(train.at[k], recv_b.at[k])
        send(*copy)

    @pl.loop(0, FSDP)
    def _(n):
        arrived(average.at[n], recv_c.at[n])

    small_done(f, t, small, gains, sems)

    @pl.loop(0, FSDP)
    def _(n):
        sent(*stage_a(n))
        sent(*stage_b(n)[1])
        sent(*stage_c(n)[1])


def exchange(kernel, wire, small, outputs, stages, collective_id):
    vmem = pl.BlockSpec(memory_space=pltpu.VMEM)
    pieces = jax.ShapeDtypeStruct(wire.shape, wire.dtype)
    dma = pltpu.SemaphoreType.DMA
    return pl.pallas_call(
        kernel,
        out_shape=[pieces] * outputs
        + [jax.ShapeDtypeStruct((FSDP, TENSOR) + small.shape, small.dtype)],
        in_specs=[vmem] * 2,
        out_specs=[vmem] * (outputs + 1),
        scratch_shapes=[pltpu.VMEM(wire.shape, wire.dtype)]
        + [dma((FSDP,))] * (2 * stages)
        + [dma((TENSOR,)), dma((TENSOR,)), dma((FSDP,)), dma((FSDP,))],
        compiler_params=pltpu.CompilerParams(
            collective_id=collective_id, has_side_effects=True
        ),
    )(wire, small)


def joined(pieces, group, layer):
    return jnp.concatenate(
        [pieces[4 * group + i, layer].astype(jnp.float32) for i in range(4)], axis=1
    )


def part(ref, buf, sem, layer, group, out):
    span = pl.ds(group * SPAN, SPAN)
    there, here = ref.at[:, layer, span], buf.at[layer, :, span]
    if out:
        there, here = here, there
    return pltpu.make_async_copy(there, here, sem.at[layer, group])


STEPS = [(layer, group) for layer in range(2) for group in range(4)]


def update_kernel(
    pieces, scale, master, first, second,
    out_wire, master_out, first_out, second_out,
    master_buf, first_buf, second_buf, *sems,
):
    cols = pieces.shape[3]
    refs = (master, first, second)
    outs = (master_out, first_out, second_out)
    bufs = (master_buf, first_buf, second_buf)
    clip_scale = scale[0, 0]
    for step in STEPS:
        for i in range(3):
            part(refs[i], bufs[i], sems[i], *step, False).start()
    for layer, group in STEPS:
        span = slice(group * SPAN, (group + 1) * SPAN)
        grads = joined(pieces, group, layer)
        for i in range(3):
            part(refs[i], bufs[i], sems[i], layer, group, False).wait()
        news = adam_step(grads, *[buf[layer, :, span] for buf in bufs], clip_scale)
        for i in range(3):
            bufs[i][layer, :, span] = news[i]
            part(outs[i], bufs[i], sems[3 + i], layer, group, True).start()
        for i in range(4):
            out_wire[4 * group + i, layer] = news[0][:, i * cols : (i + 1) * cols].astype(
                out_wire.dtype
            )
    for step in STEPS:
        for i in range(3):
            part(outs[i], bufs[i], sems[3 + i], *step, True).wait()


def average_kernel(pieces, average, average_out, buf, sem, sem_out):
    for step in STEPS:
        part(average, buf, sem, *step, False).start()
    for layer, group in STEPS:
        span = slice(group * SPAN, (group + 1) * SPAN)
        news = joined(pieces, group, layer)
        part(average, buf, sem, layer, group, False).wait()
        buf[layer, :, span] = (
            average_decay * buf[layer, :, span] + (1.0 - average_decay) * news
        )
        part(average_out, buf, sem_out, layer, group, True).start()
    for step in STEPS:
        part(average_out, buf, sem_out, *step, True).wait()


def turned(x):
    return x.transpose(1, 0, 2)


def plain(kernel, outputs, out_specs, operands, specs, states):
    shape = (2, outputs[-1].shape[0], 4 * SPAN)
    return pl.pallas_call(
        kernel,
        out_shape=outputs,
        in_specs=specs,
        out_specs=out_specs,
        scratch_shapes=[pltpu.VMEM(shape, jnp.float32)] * states
        + [pltpu.SemaphoreType.DMA((2, 4))] * (2 * states),
    )(*operands)


def on_device(
    grad_blocks,
    master_shard,
    first_moment,
    second_moment,
    average_shard,
    gain_grads,
    gain_master,
    gain_first,
    gain_second,
    gain_average,
):
    layers, block_rows, block_cols = grad_blocks.shape
    rows = block_rows // FSDP
    width = block_cols * FSDP
    entries = (grad_blocks.size + gain_grads.size) * FSDP * TENSOR

    wide = grad_blocks.astype(jnp.float32)
    gain_wide = gain_grads.astype(jnp.float32)
    squares = jnp.sum(wide * wide) + jnp.sum(gain_wide * gain_wide)
    small = jnp.pad(squares.reshape(1, 1), ((0, 0), (0, 127)))
    wire = grad_blocks.reshape(layers, FSDP, rows, block_cols).transpose(1, 0, 2, 3)
    pieces, sums = exchange(gather_kernel, wire, small, 1, 2, 0)
    total_squares = jnp.sum(sums)
    clip_scale = jnp.minimum(1.0, clip_level / jnp.sqrt(total_squares / entries + mean_epsilon))

    vmem = pl.BlockSpec(memory_space=pltpu.VMEM)
    smem = pl.BlockSpec(memory_space=pltpu.SMEM)
    far = pl.BlockSpec(memory_space=pl.ANY)
    flat = jax.ShapeDtypeStruct((rows, layers, width), jnp.float32)
    wire_out = jax.ShapeDtypeStruct(wire.shape, wire.dtype)
    out_wire, master_next, first_next, second_next = plain(
        update_kernel,
        [wire_out, flat, flat, flat],
        [vmem, far, far, far],
        (
            pieces,
            clip_scale.reshape(1, 1),
            turned(master_shard),
            turned(first_moment),
            turned(second_moment),
        ),
        [vmem, smem, far, far, far],
        3,
    )
    master_gains, first_gains, second_gains = adam_step(
        gain_grads, gain_master, gain_first, gain_second, clip_scale
    )
    average_gains = average_decay * gain_average + (1.0 - average_decay) * master_gains

    gain_count = gain_grads.size
    gain_cols = gain_grads.shape[1]
    gain_small = jnp.pad(
        master_gains.astype(jnp.bfloat16).astype(jnp.float32).reshape(1, gain_count),
        ((0, 0), (0, 128 - gain_count)),
    )
    train, averages, gains = exchange(spread_kernel, out_wire, gain_small, 2, 3, 1)
    train_weights = train.transpose(1, 0, 2, 3).reshape(layers, block_rows, block_cols)
    (average_next,) = plain(
        average_kernel, [flat], [far], (averages, turned(average_shard)), [vmem, far], 1
    )
    gain_weights = (
        gains.reshape(FSDP * TENSOR, 128)[:, :gain_count]
        .reshape(FSDP * TENSOR, layers, gain_cols)
        .transpose(1, 0, 2)
        .reshape(layers, FSDP * TENSOR * gain_cols)
        .astype(jnp.bfloat16)
    )
    return (
        train_weights,
        turned(master_next),
        turned(first_next),
        turned(second_next),
        turned(average_next),
        gain_weights,
        master_gains,
        first_gains,
        second_gains,
        average_gains,
    )


def solution(mesh):
    flat = P(None, ("fsdp", "tensor"), None)
    gain = P(None, ("fsdp", "tensor"))
    blocks = P(None, "tensor", "fsdp")
    averaging = P(None, ("tensor", "fsdp"), None)
    return jax.shard_map(
        on_device,
        mesh=mesh,
        in_specs=(blocks, flat, flat, flat, averaging, gain, gain, gain, gain, gain),
        out_specs=(blocks, flat, flat, flat, averaging, P(), gain, gain, gain, gain),
        check_vma=False,
    )
```

```python
import functools

import jax
import jax.numpy as jnp
from jax import lax
from jax.experimental import pallas as pl
from jax.experimental.pallas import tpu as pltpu
from jax.sharding import PartitionSpec as P

STEP = 20


learn_rate = 0.1
weight_decay = 0.1
beta_first = 0.9
beta_second = 0.95
adam_epsilon = 1e-08
average_decay = 0.9
clip_level = 0.5
mean_epsilon = 1e-06

MESH = pl.DeviceIdType.MESH
FSDP = 16
TENSOR = 8
LANES = 128
SPAN = 384


def adam_step(gradient, master, first_state, second_state, clip_scale):
    clipped = gradient.astype(jnp.float32) * clip_scale
    first_new = beta_first * first_state + (1.0 - beta_first) * clipped
    second_new = beta_second * second_state + (1.0 - beta_second) * clipped * clipped
    first_fix = 1.0 - beta_first**STEP
    second_fix = 1.0 - beta_second**STEP
    direction = (
        first_new / first_fix / (jnp.sqrt(second_new / second_fix) + adam_epsilon)
        + weight_decay * master
    )
    master_new = master - learn_rate * direction
    return (master_new, first_new, second_new)


def enter(f, t):
    barrier = pltpu.get_barrier_semaphore()

    @pl.loop(1, TENSOR)
    def _(i):
        pl.semaphore_signal(
            barrier, inc=1, device_id=(f, lax.rem(t + i, TENSOR)), device_id_type=MESH
        )

    @pl.loop(1, FSDP)
    def _(i):
        pl.semaphore_signal(
            barrier, inc=1, device_id=(lax.rem(f + i, FSDP), t), device_id_type=MESH
        )

    pl.semaphore_wait(barrier, TENSOR + FSDP - 2)


def remote(source, target, send_sem, recv_sem, device):
    return pltpu.make_async_remote_copy(
        src_ref=source,
        dst_ref=target,
        send_sem=send_sem,
        recv_sem=recv_sem,
        device_id=device,
        device_id_type=MESH,
    )


def send(source, target, send_sem, recv_sem, device, is_own):
    @pl.when(is_own)
    def _():
        pltpu.make_async_copy(source, target, recv_sem).start()

    @pl.when(jnp.logical_not(is_own))
    def _():
        remote(source, target, send_sem, recv_sem, device).start()


def sent(source, target, send_sem, recv_sem, device, is_own):
    @pl.when(jnp.logical_not(is_own))
    def _():
        remote(source, target, send_sem, recv_sem, device).wait_send()


def arrived(target, recv_sem):
    pltpu.make_async_copy(target, target, recv_sem).wait()


def small_copies(f, t, small_ref, all_ref, sems):
    row_send, row_recv, col_send, col_recv = sems

    def row_copy(i):
        return remote(
            small_ref,
            all_ref.at[f, t],
            row_send.at[i],
            row_recv.at[t],
            (f, lax.rem(t + i, TENSOR)),
        )

    def col_copy(i):
        return remote(
            all_ref.at[f],
            all_ref.at[f],
            col_send.at[i],
            col_recv.at[f],
            (lax.rem(f + i, FSDP), t),
        )

    return row_copy, col_copy


def small_first(f, t, small_ref, all_ref, sems):
    row_copy, _ = small_copies(f, t, small_ref, all_ref, sems)
    pltpu.make_async_copy(small_ref, all_ref.at[f, t], sems[1].at[t]).start()

    @pl.loop(1, TENSOR)
    def _(i):
        row_copy(i).start()


def small_second(f, t, small_ref, all_ref, sems):
    _, col_copy = small_copies(f, t, small_ref, all_ref, sems)

    @pl.loop(0, TENSOR)
    def _(i):
        arrived(all_ref.at[f, i], sems[1].at[i])

    @pl.loop(1, FSDP)
    def _(i):
        col_copy(i).start()


def small_done(f, t, small_ref, all_ref, sems):
    row_copy, col_copy = small_copies(f, t, small_ref, all_ref, sems)

    @pl.loop(1, FSDP)
    def _(i):
        source = lax.rem(f + i, FSDP)
        arrived(all_ref.at[source], sems[3].at[source])

    @pl.loop(1, TENSOR)
    def _(i):
        row_copy(i).wait_send()

    @pl.loop(1, FSDP)
    def _(i):
        col_copy(i).wait_send()


def gather_kernel(
    wire, small, out, sums, mid, send_a, recv_a, send_b, recv_b, rs, rr, cs, cr
):
    f = lax.axis_index("fsdp")
    t = lax.axis_index("tensor")
    sems = (rs, rr, cs, cr)
    enter(f, t)
    small_first(f, t, small, sums, sems)
    small_second(f, t, small, sums, sems)

    def stage_a(n):
        i, half = n // 2, lax.rem(n + f // TENSOR, 2)
        to = lax.rem(t + i + f, TENSOR)
        k = half * TENSOR + to
        slot = 2 * t + half
        return (
            wire.at[k], mid.at[slot], send_a.at[k], recv_a.at[slot], (f, to), to == t,
        )

    def stage_b(n):
        i, half = n // 2, lax.rem(n + f // TENSOR, 2)
        m = 2 * lax.rem(t - i - f + 4 * TENSOR, TENSOR) + half
        return m, (mid.at[m], out.at[f], send_b.at[m], recv_b.at[f], (m, t), m == f)

    @pl.loop(0, FSDP)
    def _(n):
        send(*stage_a(n))

    @pl.loop(0, FSDP)
    def _(n):
        m, copy = stage_b(n)
        arrived(mid.at[m], recv_a.at[m])
        send(*copy)

    @pl.loop(0, FSDP)
    def _(n):
        arrived(out.at[n], recv_b.at[n])

    small_done(f, t, small, sums, sems)

    @pl.loop(0, FSDP)
    def _(n):
        sent(*stage_a(n))
        sent(*stage_b(n)[1])


def spread_kernel(
    wire, small, train, average, gains, mid,
    send_a, recv_a, send_b, recv_b, send_c, recv_c, rs, rr, cs, cr,
):
    f = lax.axis_index("fsdp")
    t = lax.axis_index("tensor")
    sems = (rs, rr, cs, cr)
    enter(f, t)
    small_first(f, t, small, gains, sems)

    def stage_a(n):
        j = lax.rem(f + n + 2 * t, FSDP)
        return (wire.at[j], mid.at[f], send_a.at[j], recv_a.at[f], (j, t), j == f)

    def stage_b(n):
        source = lax.rem(f - n - 2 * t + 2 * FSDP, FSDP)
        to = source // 2
        k = lax.rem(source, 2) * TENSOR + t
        return source, (
            mid.at[source], train.at[k], send_b.at[source], recv_b.at[k], (f, to), to == t,
        )

    def stage_c(n):
        k = lax.rem(n, 2) * TENSOR + lax.rem(n // 2 + f + t, TENSOR)
        return k, (train.at[k], average.at[f], send_c.at[k], recv_c.at[f], (k, t), k == f)

    @pl.loop(0, FSDP)
    def _(n):
        send(*stage_a(n))

    @pl.loop(0, FSDP)
    def _(n):
        source, copy = stage_b(n)
        arrived(mid.at[source], recv_a.at[source])
        send(*copy)

    small_second(f, t, small, gains, sems)

    @pl.loop(0, FSDP)
    def _(n):
        k, copy = stage_c(n)
        arrived(train.at[k], recv_b.at[k])
        send(*copy)

    @pl.loop(0, FSDP)
    def _(n):
        arrived(average.at[n], recv_c.at[n])

    small_done(f, t, small, gains, sems)

    @pl.loop(0, FSDP)
    def _(n):
        sent(*stage_a(n))
        sent(*stage_b(n)[1])
        sent(*stage_c(n)[1])


def exchange(kernel, wire, small, outputs, stages, collective_id):
    vmem = pl.BlockSpec(memory_space=pltpu.VMEM)
    pieces = jax.ShapeDtypeStruct(wire.shape, wire.dtype)
    dma = pltpu.SemaphoreType.DMA
    return pl.pallas_call(
        kernel,
        out_shape=[pieces] * outputs
        + [jax.ShapeDtypeStruct((FSDP, TENSOR) + small.shape, small.dtype)],
        in_specs=[vmem] * 2,
        out_specs=[vmem] * (outputs + 1),
        scratch_shapes=[pltpu.VMEM(wire.shape, wire.dtype)]
        + [dma((FSDP,))] * (2 * stages)
        + [dma((TENSOR,)), dma((TENSOR,)), dma((FSDP,)), dma((FSDP,))],
        compiler_params=pltpu.CompilerParams(
            collective_id=collective_id, has_side_effects=True
        ),
    )(wire, small)


def total(x):
    wide = x.astype(jnp.float32)
    return jnp.sum(jnp.sum(wide * wide, axis=0, keepdims=True), axis=1, keepdims=True)


def same(shape, shift):
    i = lax.broadcasted_iota(jnp.int32, shape, 0)
    j = lax.broadcasted_iota(jnp.int32, shape, 1)
    return jnp.where(j == i + shift, 1.0, 0.0).astype(jnp.bfloat16)


def turn(a, b):
    return lax.dot_general(
        a, b, (((1,), (1,)), ((), ())), preferred_element_type=jnp.float32
    )


def prepare_kernel(blocks, gains, wire, small):
    layers, _, block_rows = blocks.shape
    rows = wire.shape[2]
    for k in range(FSDP):
        start = rows * k // LANES * LANES
        size = min(2 * LANES, block_rows - start)
        chosen = same((rows, size), rows * k - start)
        for layer in range(layers):
            wire[k, layer] = turn(chosen, blocks[layer, :, pl.ds(start, size)]).astype(
                wire.dtype
            )
    squares = total(gains[...])
    for layer in range(layers):
        squares += total(blocks[layer])
    lane = lax.broadcasted_iota(jnp.int32, small.shape, 1)
    small[...] = jnp.where(lane == 0, squares, 0.0)


def joined(pieces, group, layer):
    return jnp.concatenate(
        [pieces[4 * group + i, layer].astype(jnp.float32) for i in range(4)], axis=1
    )


def part(ref, buf, sem, layer, group, out):
    span = pl.ds(group * SPAN, SPAN)
    there, here = ref.at[:, layer, span], buf.at[layer, :, span]
    if out:
        there, here = here, there
    return pltpu.make_async_copy(there, here, sem.at[layer, group])


STEPS = [(layer, group) for layer in range(2) for group in range(4)]


def update_kernel(
    entries, pieces, sums, gain_grads, gain_master, gain_first, gain_second, gain_average,
    master, first, second,
    out_wire, gain_master_out, gain_first_out, gain_second_out, gain_average_out,
    master_out, first_out, second_out,
    master_buf, first_buf, second_buf, *sems,
):
    cols = pieces.shape[3]
    refs = (master, first, second)
    outs = (master_out, first_out, second_out)
    bufs = (master_buf, first_buf, second_buf)
    for step in STEPS:
        for i in range(3):
            part(refs[i], bufs[i], sems[i], *step, False).start()
    squares = jnp.sum(jnp.sum(sums[...], axis=0, keepdims=True), axis=1, keepdims=True)
    clip_scale = jnp.minimum(1.0, clip_level / jnp.sqrt(squares / entries + mean_epsilon))
    gain_news = adam_step(
        gain_grads[...], gain_master[...], gain_first[...], gain_second[...], clip_scale
    )
    gain_master_out[...], gain_first_out[...], gain_second_out[...] = gain_news
    gain_average_out[...] = (
        average_decay * gain_average[...] + (1.0 - average_decay) * gain_news[0]
    )
    for layer, group in STEPS:
        span = slice(group * SPAN, (group + 1) * SPAN)
        grads = joined(pieces, group, layer)
        for i in range(3):
            part(refs[i], bufs[i], sems[i], layer, group, False).wait()
        news = adam_step(grads, *[buf[layer, :, span] for buf in bufs], clip_scale)
        for i in range(3):
            bufs[i][layer, :, span] = news[i]
            part(outs[i], bufs[i], sems[3 + i], layer, group, True).start()
        for i in range(4):
            out_wire[4 * group + i, layer] = news[0][:, i * cols : (i + 1) * cols].astype(
                out_wire.dtype
            )
    for step in STEPS:
        for i in range(3):
            part(outs[i], bufs[i], sems[3 + i], *step, True).wait()


def finish_kernel(
    train, pieces, average, train_out, average_out, buf, sem, sem_out, stack
):
    for step in STEPS:
        part(average, buf, sem, *step, False).start()
    for layer, group in STEPS:
        span = slice(group * SPAN, (group + 1) * SPAN)
        news = joined(pieces, group, layer)
        part(average, buf, sem, layer, group, False).wait()
        buf[layer, :, span] = (
            average_decay * buf[layer, :, span] + (1.0 - average_decay) * news
        )
        part(average_out, buf, sem_out, layer, group, True).start()
    layers, cols, block_rows = train_out.shape
    rows = train.shape[2]
    unit = same((cols, cols), 0)
    for layer in range(layers):
        for k in range(FSDP):
            stack[pl.ds(rows * k, rows), :] = train[k, layer].astype(jnp.float32)
        for start in range(0, block_rows, 2 * LANES):
            size = min(2 * LANES, block_rows - start)
            here = pl.ds(start, size)
            train_out[layer, :, here] = turn(
                unit, stack[here, :].astype(jnp.bfloat16)
            ).astype(train_out.dtype)
    for step in STEPS:
        part(average_out, buf, sem_out, *step, True).wait()


def turned(x):
    return x.transpose(1, 0, 2)


def plain(kernel, outputs, out_specs, operands, specs, states, scratch=()):
    shape = (2, outputs[-1].shape[0], 4 * SPAN)
    return pl.pallas_call(
        kernel,
        out_shape=outputs,
        in_specs=specs,
        out_specs=out_specs,
        scratch_shapes=[pltpu.VMEM(shape, jnp.float32)] * states
        + [pltpu.SemaphoreType.DMA((2, 4))] * (2 * states)
        + list(scratch),
    )(*operands)


def on_device(
    grad_blocks,
    master_shard,
    first_moment,
    second_moment,
    average_shard,
    gain_grads,
    gain_master,
    gain_first,
    gain_second,
    gain_average,
):
    layers, block_rows, block_cols = grad_blocks.shape
    rows = block_rows // FSDP
    width = block_cols * FSDP
    entries = (grad_blocks.size + gain_grads.size) * FSDP * TENSOR

    vmem = pl.BlockSpec(memory_space=pltpu.VMEM)
    far = pl.BlockSpec(memory_space=pl.ANY)
    one_row = jax.ShapeDtypeStruct((1, LANES), jnp.float32)
    wire_shape = jax.ShapeDtypeStruct((FSDP, layers, rows, block_cols), grad_blocks.dtype)
    flat = jax.ShapeDtypeStruct((rows, layers, width), jnp.float32)
    gain = jax.ShapeDtypeStruct(gain_master.shape, jnp.float32)

    wire, small = pl.pallas_call(
        prepare_kernel,
        out_shape=[wire_shape, one_row],
        in_specs=[vmem] * 2,
        out_specs=[vmem] * 2,
    )(grad_blocks.transpose(0, 2, 1), gain_grads)
    pieces, sums = exchange(gather_kernel, wire, small, 1, 2, 0)

    (
        out_wire,
        master_gains,
        first_gains,
        second_gains,
        average_gains,
        master_next,
        first_next,
        second_next,
    ) = plain(
        functools.partial(update_kernel, entries),
        [wire_shape] + [gain] * 4 + [flat] * 3,
        [vmem] * 5 + [far] * 3,
        (
            pieces,
            sums.reshape(FSDP * TENSOR, LANES),
            gain_grads,
            gain_master,
            gain_first,
            gain_second,
            gain_average,
            turned(master_shard),
            turned(first_moment),
            turned(second_moment),
        ),
        [vmem] * 7 + [far] * 3,
        3,
    )
    train, averages, gains = exchange(spread_kernel, out_wire, master_gains, 2, 3, 1)
    train_turned, average_next = plain(
        finish_kernel,
        [jax.ShapeDtypeStruct((layers, block_cols, block_rows), jnp.bfloat16), flat],
        [vmem, far],
        (train, averages, turned(average_shard)),
        [vmem, vmem, far],
        1,
        [pltpu.VMEM((block_rows, block_cols), jnp.float32)],
    )
    train_weights = train_turned.transpose(0, 2, 1)
    gain_weights = (
        gains.astype(jnp.bfloat16).transpose(2, 0, 1, 3).reshape(layers, -1)
    )
    return (
        train_weights,
        turned(master_next),
        turned(first_next),
        turned(second_next),
        turned(average_next),
        gain_weights,
        master_gains,
        first_gains,
        second_gains,
        average_gains,
    )


def solution(mesh):
    flat = P(None, ("fsdp", "tensor"), None)
    gain = P(None, ("fsdp", "tensor"))
    blocks = P(None, "tensor", "fsdp")
    averaging = P(None, ("tensor", "fsdp"), None)
    return jax.shard_map(
        on_device,
        mesh=mesh,
        in_specs=(blocks, flat, flat, flat, averaging, gain, gain, gain, gain, gain),
        out_specs=(blocks, flat, flat, flat, averaging, P(), gain, gain, gain, gain),
        check_vma=False,
    )
```

```python
import functools

import jax
import jax.numpy as jnp
from jax import lax
from jax.experimental import pallas as pl
from jax.experimental.pallas import tpu as pltpu
from jax.sharding import PartitionSpec as P

STEP = 20


learn_rate = 0.1
weight_decay = 0.1
beta_first = 0.9
beta_second = 0.95
adam_epsilon = 1e-08
average_decay = 0.9
clip_level = 0.5
mean_epsilon = 1e-06

MESH = pl.DeviceIdType.MESH
FSDP = 16
TENSOR = 8
LANES = 128
SPAN = 384


def adam_step(gradient, master, first_state, second_state, clip_scale):
    clipped = gradient.astype(jnp.float32) * clip_scale
    first_new = beta_first * first_state + (1.0 - beta_first) * clipped
    second_new = beta_second * second_state + (1.0 - beta_second) * clipped * clipped
    first_fix = 1.0 - beta_first**STEP
    second_fix = 1.0 - beta_second**STEP
    direction = (
        first_new / first_fix / (jnp.sqrt(second_new / second_fix) + adam_epsilon)
        + weight_decay * master
    )
    master_new = master - learn_rate * direction
    return (master_new, first_new, second_new)


def enter(f, t):
    barrier = pltpu.get_barrier_semaphore()

    @pl.loop(1, TENSOR)
    def _(i):
        pl.semaphore_signal(
            barrier, inc=1, device_id=(f, lax.rem(t + i, TENSOR)), device_id_type=MESH
        )

    @pl.loop(1, FSDP)
    def _(i):
        pl.semaphore_signal(
            barrier, inc=1, device_id=(lax.rem(f + i, FSDP), t), device_id_type=MESH
        )

    pl.semaphore_wait(barrier, TENSOR + FSDP - 2)


def remote(source, target, send_sem, recv_sem, device):
    return pltpu.make_async_remote_copy(
        src_ref=source,
        dst_ref=target,
        send_sem=send_sem,
        recv_sem=recv_sem,
        device_id=device,
        device_id_type=MESH,
    )


def send(source, target, send_sem, recv_sem, device, is_own):
    @pl.when(is_own)
    def _():
        pltpu.make_async_copy(source, target, recv_sem).start()

    @pl.when(jnp.logical_not(is_own))
    def _():
        remote(source, target, send_sem, recv_sem, device).start()


def sent(source, target, send_sem, recv_sem, device, is_own):
    @pl.when(jnp.logical_not(is_own))
    def _():
        remote(source, target, send_sem, recv_sem, device).wait_send()


def arrived(target, recv_sem):
    pltpu.make_async_copy(target, target, recv_sem).wait()


def small_copies(f, t, small_ref, all_ref, sems):
    row_send, row_recv, col_send, col_recv = sems

    def row_copy(i):
        return remote(
            small_ref,
            all_ref.at[f, t],
            row_send.at[i],
            row_recv.at[t],
            (f, lax.rem(t + i, TENSOR)),
        )

    def col_copy(i):
        return remote(
            all_ref.at[f],
            all_ref.at[f],
            col_send.at[i],
            col_recv.at[f],
            (lax.rem(f + i, FSDP), t),
        )

    return row_copy, col_copy


def small_first(f, t, small_ref, all_ref, sems):
    row_copy, _ = small_copies(f, t, small_ref, all_ref, sems)
    pltpu.make_async_copy(small_ref, all_ref.at[f, t], sems[1].at[t]).start()

    @pl.loop(1, TENSOR)
    def _(i):
        row_copy(i).start()


def small_second(f, t, small_ref, all_ref, sems):
    _, col_copy = small_copies(f, t, small_ref, all_ref, sems)

    @pl.loop(0, TENSOR)
    def _(i):
        arrived(all_ref.at[f, i], sems[1].at[i])

    @pl.loop(1, FSDP)
    def _(i):
        col_copy(i).start()


def small_done(f, t, small_ref, all_ref, sems):
    row_copy, col_copy = small_copies(f, t, small_ref, all_ref, sems)

    @pl.loop(1, FSDP)
    def _(i):
        source = lax.rem(f + i, FSDP)
        arrived(all_ref.at[source], sems[3].at[source])

    @pl.loop(1, TENSOR)
    def _(i):
        row_copy(i).wait_send()

    @pl.loop(1, FSDP)
    def _(i):
        col_copy(i).wait_send()


def gather_kernel(
    wire, small, out, sums, mid, send_a, recv_a, send_b, recv_b, rs, rr, cs, cr
):
    f = lax.axis_index("fsdp")
    t = lax.axis_index("tensor")
    sems = (rs, rr, cs, cr)
    enter(f, t)
    small_first(f, t, small, sums, sems)

    def stage_a(n):
        i, half = n // 2, lax.rem(n + f // TENSOR, 2)
        to = lax.rem(t + i + f, TENSOR)
        k = half * TENSOR + to
        slot = 2 * t + half
        return (
            wire.at[k], mid.at[slot], send_a.at[k], recv_a.at[slot], (f, to), to == t,
        )

    def stage_b(n):
        i, half = n // 2, lax.rem(n + f // TENSOR, 2)
        m = 2 * lax.rem(t - i - f + 4 * TENSOR, TENSOR) + half
        return m, (mid.at[m], out.at[f], send_b.at[m], recv_b.at[f], (m, t), m == f)

    @pl.loop(0, FSDP)
    def _(n):
        send(*stage_a(n))

    small_second(f, t, small, sums, sems)

    @pl.loop(0, FSDP)
    def _(n):
        m, copy = stage_b(n)
        arrived(mid.at[m], recv_a.at[m])
        send(*copy)

    @pl.loop(0, FSDP)
    def _(n):
        arrived(out.at[n], recv_b.at[n])

    small_done(f, t, small, sums, sems)

    @pl.loop(0, FSDP)
    def _(n):
        sent(*stage_a(n))
        sent(*stage_b(n)[1])


def spread_kernel(
    wire, small, train, average, gains, mid,
    send_a, recv_a, send_b, recv_b, send_c, recv_c, rs, rr, cs, cr,
):
    f = lax.axis_index("fsdp")
    t = lax.axis_index("tensor")
    sems = (rs, rr, cs, cr)
    enter(f, t)
    small_first(f, t, small, gains, sems)

    def stage_a(n):
        j = lax.rem(f + n + 2 * t, FSDP)
        return (wire.at[j], mid.at[f], send_a.at[j], recv_a.at[f], (j, t), j == f)

    def stage_b(n):
        source = lax.rem(f - n - 2 * t + 2 * FSDP, FSDP)
        to = source // 2
        k = lax.rem(source, 2) * TENSOR + t
        return source, (
            mid.at[source], train.at[k], send_b.at[source], recv_b.at[k], (f, to), to == t,
        )

    def stage_c(n):
        k = lax.rem(n, 2) * TENSOR + lax.rem(n // 2 + f + t, TENSOR)
        return k, (train.at[k], average.at[f], send_c.at[k], recv_c.at[f], (k, t), k == f)

    @pl.loop(0, FSDP)
    def _(n):
        send(*stage_a(n))

    @pl.loop(0, FSDP)
    def _(n):
        source, copy = stage_b(n)
        arrived(mid.at[source], recv_a.at[source])
        send(*copy)

    small_second(f, t, small, gains, sems)

    @pl.loop(0, FSDP)
    def _(n):
        k, copy = stage_c(n)
        arrived(train.at[k], recv_b.at[k])
        send(*copy)

    @pl.loop(0, FSDP)
    def _(n):
        arrived(average.at[n], recv_c.at[n])

    small_done(f, t, small, gains, sems)

    @pl.loop(0, FSDP)
    def _(n):
        sent(*stage_a(n))
        sent(*stage_b(n)[1])
        sent(*stage_c(n)[1])


def exchange(kernel, wire, small, outputs, stages, collective_id):
    vmem = pl.BlockSpec(memory_space=pltpu.VMEM)
    pieces = jax.ShapeDtypeStruct(wire.shape, wire.dtype)
    dma = pltpu.SemaphoreType.DMA
    return pl.pallas_call(
        kernel,
        out_shape=[pieces] * outputs
        + [jax.ShapeDtypeStruct((FSDP, TENSOR) + small.shape, small.dtype)],
        in_specs=[vmem] * 2,
        out_specs=[vmem] * (outputs + 1),
        scratch_shapes=[pltpu.VMEM(wire.shape, wire.dtype)]
        + [dma((FSDP,))] * (2 * stages)
        + [dma((TENSOR,)), dma((TENSOR,)), dma((FSDP,)), dma((FSDP,))],
        compiler_params=pltpu.CompilerParams(
            collective_id=collective_id, has_side_effects=True
        ),
    )(wire, small)


def total(x):
    wide = x.astype(jnp.float32)
    return jnp.sum(jnp.sum(wide * wide, axis=0, keepdims=True), axis=1, keepdims=True)


def same(shape, shift):
    i = lax.broadcasted_iota(jnp.int32, shape, 0)
    j = lax.broadcasted_iota(jnp.int32, shape, 1)
    return jnp.where(j == i + shift, 1.0, 0.0).astype(jnp.bfloat16)


def turn(a, b):
    return lax.dot_general(
        a, b, (((1,), (1,)), ((), ())), preferred_element_type=jnp.float32
    )


def put_tails(wire, k, tails):
    count, cols = tails.shape
    full = jnp.concatenate([tails, jnp.zeros((count, LANES - cols), jnp.float32)], axis=1)
    wire[k, pl.ds(wire.shape[1] - count, count), :] = full.astype(wire.dtype)


def unpack(pieces, k, layer, cols, unit):
    rest = pieces.shape[1] // 2 - cols
    head = turn(unit, pieces[k, pl.ds(layer * cols, cols), :])
    tails = pieces[k, pl.ds(2 * cols, 2 * rest), :].astype(jnp.float32)
    return jnp.concatenate([head, tails[layer * rest : (layer + 1) * rest, :cols]], axis=0)


def prepare_kernel(blocks, gains, wire, small):
    layers, cols, block_rows = blocks.shape
    rows = block_rows // FSDP
    rest = rows - LANES
    for k in range(FSDP):
        start = rows * k // LANES * LANES
        size = min(2 * LANES, block_rows - start)
        shift = rows * k - start
        chosen = same((LANES, size), shift)
        tails = jnp.zeros((layers * rest, cols), jnp.float32)
        for layer in range(layers):
            window = blocks[layer, :, pl.ds(start, size)]
            wire[k, pl.ds(layer * cols, cols), :] = turn(window, chosen).astype(wire.dtype)
            i = lax.broadcasted_iota(jnp.int32, (layers * rest, size), 0) - layer * rest
            j = lax.broadcasted_iota(jnp.int32, (layers * rest, size), 1) - shift - LANES
            hit = (i == j) & (i >= 0) & (i < rest)
            tails += turn(jnp.where(hit, 1.0, 0.0).astype(window.dtype), window)
        put_tails(wire, k, tails)
    squares = total(gains[...])
    for layer in range(layers):
        squares += total(blocks[layer])
    lane = lax.broadcasted_iota(jnp.int32, small.shape, 1)
    small[...] = jnp.where(lane == 0, squares, 0.0)


def joined(pieces, group, layer, unit):
    return jnp.concatenate(
        [unpack(pieces, 4 * group + i, layer, SPAN // 4, unit) for i in range(4)], axis=1
    )


def part(ref, buf, sem, layer, group, out):
    span = pl.ds(group * SPAN, SPAN)
    there, here = ref.at[:, layer, span], buf.at[layer, :, span]
    if out:
        there, here = here, there
    return pltpu.make_async_copy(there, here, sem.at[layer, group])


STEPS = [(layer, group) for group in range(4) for layer in range(2)]


def update_kernel(
    entries, pieces, sums, gain_grads, gain_master, gain_first, gain_second, gain_average,
    master, first, second,
    out_wire, gain_master_out, gain_first_out, gain_second_out, gain_average_out,
    master_out, first_out, second_out,
    master_buf, first_buf, second_buf, *sems,
):
    cols = SPAN // 4
    unit = same((LANES, LANES), 0)
    unit_cols = same((cols, cols), 0)
    tails = {}
    refs = (master, first, second)
    outs = (master_out, first_out, second_out)
    bufs = (master_buf, first_buf, second_buf)
    for step in STEPS:
        for i in range(3):
            part(refs[i], bufs[i], sems[i], *step, False).start()
    squares = jnp.sum(jnp.sum(sums[...], axis=0, keepdims=True), axis=1, keepdims=True)
    clip_scale = jnp.minimum(1.0, clip_level / jnp.sqrt(squares / entries + mean_epsilon))
    gain_news = adam_step(
        gain_grads[...], gain_master[...], gain_first[...], gain_second[...], clip_scale
    )
    gain_master_out[...], gain_first_out[...], gain_second_out[...] = gain_news
    gain_average_out[...] = (
        average_decay * gain_average[...] + (1.0 - average_decay) * gain_news[0]
    )
    for layer, group in STEPS:
        span = slice(group * SPAN, (group + 1) * SPAN)
        grads = joined(pieces, group, layer, unit)
        for i in range(3):
            part(refs[i], bufs[i], sems[i], layer, group, False).wait()
        news = adam_step(grads, *[buf[layer, :, span] for buf in bufs], clip_scale)
        for i in range(3):
            bufs[i][layer, :, span] = news[i]
            part(outs[i], bufs[i], sems[3 + i], layer, group, True).start()
        for i in range(4):
            piece = news[0][:, i * cols : (i + 1) * cols]
            out_wire[4 * group + i, pl.ds(layer * cols, cols), :] = turn(
                unit_cols, piece[:LANES].astype(out_wire.dtype)
            ).astype(out_wire.dtype)
            tails[i, layer] = piece[LANES:]
        if layer == 1:
            for i in range(4):
                both = jnp.concatenate([tails[i, 0], tails[i, 1]], axis=0)
                put_tails(out_wire, 4 * group + i, both)
    for step in STEPS:
        for i in range(3):
            part(outs[i], bufs[i], sems[3 + i], *step, True).wait()


def finish_kernel(
    train, pieces, average, train_out, average_out, buf, sem, sem_out, stack
):
    for step in STEPS:
        part(average, buf, sem, *step, False).start()
    unit = same((LANES, LANES), 0)
    for layer, group in STEPS:
        span = slice(group * SPAN, (group + 1) * SPAN)
        news = joined(pieces, group, layer, unit)
        part(average, buf, sem, layer, group, False).wait()
        buf[layer, :, span] = (
            average_decay * buf[layer, :, span] + (1.0 - average_decay) * news
        )
        part(average_out, buf, sem_out, layer, group, True).start()
    layers, cols, block_rows = train_out.shape
    rows = block_rows // FSDP
    unit_cols = same((cols, cols), 0)
    for layer in range(layers):
        for k in range(FSDP):
            stack[pl.ds(rows * k, rows), :] = unpack(train, k, layer, cols, unit)
        for start in range(0, block_rows, 2 * LANES):
            size = min(2 * LANES, block_rows - start)
            here = pl.ds(start, size)
            train_out[layer, :, here] = turn(
                unit_cols, stack[here, :].astype(jnp.bfloat16)
            ).astype(train_out.dtype)
    for step in STEPS:
        part(average_out, buf, sem_out, *step, True).wait()


def turned(x):
    return x.transpose(1, 0, 2)


def plain(kernel, outputs, out_specs, operands, specs, states, scratch=()):
    shape = (2, outputs[-1].shape[0], 4 * SPAN)
    return pl.pallas_call(
        kernel,
        out_shape=outputs,
        in_specs=specs,
        out_specs=out_specs,
        scratch_shapes=[pltpu.VMEM(shape, jnp.float32)] * states
        + [pltpu.SemaphoreType.DMA((2, 4))] * (2 * states)
        + list(scratch),
    )(*operands)


def on_device(
    grad_blocks,
    master_shard,
    first_moment,
    second_moment,
    average_shard,
    gain_grads,
    gain_master,
    gain_first,
    gain_second,
    gain_average,
):
    layers, block_rows, block_cols = grad_blocks.shape
    rows = block_rows // FSDP
    width = block_cols * FSDP
    entries = (grad_blocks.size + gain_grads.size) * FSDP * TENSOR

    vmem = pl.BlockSpec(memory_space=pltpu.VMEM)
    far = pl.BlockSpec(memory_space=pl.ANY)
    one_row = jax.ShapeDtypeStruct((1, LANES), jnp.float32)
    dense = layers * (block_cols + rows - LANES)
    wire_shape = jax.ShapeDtypeStruct((FSDP, dense, LANES), grad_blocks.dtype)
    flat = jax.ShapeDtypeStruct((rows, layers, width), jnp.float32)
    gain = jax.ShapeDtypeStruct(gain_master.shape, jnp.float32)

    wire, small = pl.pallas_call(
        prepare_kernel,
        out_shape=[wire_shape, one_row],
        in_specs=[vmem] * 2,
        out_specs=[vmem] * 2,
    )(grad_blocks.transpose(0, 2, 1), gain_grads)
    pieces, sums = exchange(gather_kernel, wire, small, 1, 2, 0)

    (
        out_wire,
        master_gains,
        first_gains,
        second_gains,
        average_gains,
        master_next,
        first_next,
        second_next,
    ) = plain(
        functools.partial(update_kernel, entries),
        [wire_shape] + [gain] * 4 + [flat] * 3,
        [vmem] * 5 + [far] * 3,
        (
            pieces,
            sums.reshape(FSDP * TENSOR, LANES),
            gain_grads,
            gain_master,
            gain_first,
            gain_second,
            gain_average,
            turned(master_shard),
            turned(first_moment),
            turned(second_moment),
        ),
        [vmem] * 7 + [far] * 3,
        3,
    )
    train, averages, gains = exchange(spread_kernel, out_wire, master_gains, 2, 3, 1)
    train_turned, average_next = plain(
        finish_kernel,
        [jax.ShapeDtypeStruct((layers, block_cols, block_rows), jnp.bfloat16), flat],
        [vmem, far],
        (train, averages, turned(average_shard)),
        [vmem, vmem, far],
        1,
        [pltpu.VMEM((block_rows, block_cols), jnp.float32)],
    )
    train_weights = train_turned.transpose(0, 2, 1)
    gain_weights = (
        gains.astype(jnp.bfloat16).transpose(2, 0, 1, 3).reshape(layers, -1)
    )
    return (
        train_weights,
        turned(master_next),
        turned(first_next),
        turned(second_next),
        turned(average_next),
        gain_weights,
        master_gains,
        first_gains,
        second_gains,
        average_gains,
    )


def solution(mesh):
    flat = P(None, ("fsdp", "tensor"), None)
    gain = P(None, ("fsdp", "tensor"))
    blocks = P(None, "tensor", "fsdp")
    averaging = P(None, ("tensor", "fsdp"), None)
    return jax.shard_map(
        on_device,
        mesh=mesh,
        in_specs=(blocks, flat, flat, flat, averaging, gain, gain, gain, gain, gain),
        out_specs=(blocks, flat, flat, flat, averaging, P(), gain, gain, gain, gain),
        check_vma=False,
    )
```

```python
import functools

import jax
import jax.numpy as jnp
from jax import lax
from jax.experimental import pallas as pl
from jax.experimental.pallas import tpu as pltpu
from jax.sharding import PartitionSpec as P

STEP = 20


learn_rate = 0.1
weight_decay = 0.1
beta_first = 0.9
beta_second = 0.95
adam_epsilon = 1e-08
average_decay = 0.9
clip_level = 0.5
mean_epsilon = 1e-06

MESH = pl.DeviceIdType.MESH
FSDP = 16
TENSOR = 8
LANES = 128
SPAN = 384


def adam_step(gradient, master, first_state, second_state, clip_scale):
    clipped = gradient.astype(jnp.float32) * clip_scale
    first_new = beta_first * first_state + (1.0 - beta_first) * clipped
    second_new = beta_second * second_state + (1.0 - beta_second) * clipped * clipped
    first_fix = 1.0 - beta_first**STEP
    second_fix = 1.0 - beta_second**STEP
    direction = (
        first_new / first_fix / (jnp.sqrt(second_new / second_fix) + adam_epsilon)
        + weight_decay * master
    )
    master_new = master - learn_rate * direction
    return (master_new, first_new, second_new)


def enter(f, t, sources=None):
    barrier = pltpu.get_barrier_semaphore()

    @pl.loop(1, TENSOR)
    def _(i):
        pl.semaphore_signal(
            barrier, inc=1, device_id=(f, lax.rem(t + i, TENSOR)), device_id_type=MESH
        )

    @pl.loop(1, FSDP)
    def _(i):
        pl.semaphore_signal(
            barrier, inc=1, device_id=(lax.rem(f + i, FSDP), t), device_id_type=MESH
        )

    peers = TENSOR + FSDP - 2
    if sources is not None:
        peers += FSDP - (f // 2 == t).astype(jnp.int32)

        @pl.loop(0, FSDP)
        def _(i):
            source_f, source_t = sources(i)

            @pl.when(jnp.logical_not((source_f == f) & (source_t == t)))
            def _():
                pl.semaphore_signal(
                    barrier, inc=1, device_id=(source_f, source_t), device_id_type=MESH
                )

    pl.semaphore_wait(barrier, peers)


def remote(source, target, send_sem, recv_sem, device):
    return pltpu.make_async_remote_copy(
        src_ref=source,
        dst_ref=target,
        send_sem=send_sem,
        recv_sem=recv_sem,
        device_id=device,
        device_id_type=MESH,
    )


def send(source, target, send_sem, recv_sem, device, is_own):
    @pl.when(is_own)
    def _():
        pltpu.make_async_copy(source, target, recv_sem).start()

    @pl.when(jnp.logical_not(is_own))
    def _():
        remote(source, target, send_sem, recv_sem, device).start()


def sent(source, target, send_sem, recv_sem, device, is_own):
    @pl.when(jnp.logical_not(is_own))
    def _():
        remote(source, target, send_sem, recv_sem, device).wait_send()


def arrived(target, recv_sem):
    pltpu.make_async_copy(target, target, recv_sem).wait()


def small_copies(f, t, small_ref, all_ref, sems):
    row_send, row_recv, col_send, col_recv = sems

    def row_copy(i):
        return remote(
            small_ref,
            all_ref.at[f, t],
            row_send.at[i],
            row_recv.at[t],
            (f, lax.rem(t + i, TENSOR)),
        )

    def col_copy(i):
        return remote(
            all_ref.at[f],
            all_ref.at[f],
            col_send.at[i],
            col_recv.at[f],
            (lax.rem(f + i, FSDP), t),
        )

    return row_copy, col_copy


def small_first(f, t, small_ref, all_ref, sems):
    row_copy, _ = small_copies(f, t, small_ref, all_ref, sems)
    pltpu.make_async_copy(small_ref, all_ref.at[f, t], sems[1].at[t]).start()

    @pl.loop(1, TENSOR)
    def _(i):
        row_copy(i).start()


def small_second(f, t, small_ref, all_ref, sems):
    _, col_copy = small_copies(f, t, small_ref, all_ref, sems)

    @pl.loop(0, TENSOR)
    def _(i):
        arrived(all_ref.at[f, i], sems[1].at[i])

    @pl.loop(1, FSDP)
    def _(i):
        col_copy(i).start()


def small_done(f, t, small_ref, all_ref, sems):
    row_copy, col_copy = small_copies(f, t, small_ref, all_ref, sems)

    @pl.loop(1, FSDP)
    def _(i):
        source = lax.rem(f + i, FSDP)
        arrived(all_ref.at[source], sems[3].at[source])

    @pl.loop(1, TENSOR)
    def _(i):
        row_copy(i).wait_send()

    @pl.loop(1, FSDP)
    def _(i):
        col_copy(i).wait_send()


def gather_kernel(wire, small, out, sums, send_a, recv_a, rs, rr, cs, cr):
    f = lax.axis_index("fsdp")
    t = lax.axis_index("tensor")
    sems = (rs, rr, cs, cr)
    enter(f, t, lambda i: (i, f // 2))
    small_first(f, t, small, sums, sems)
    small_second(f, t, small, sums, sems)

    def stage_a(n):
        half = lax.rem(n + f // TENSOR, 2)
        to = lax.rem(t + n // 2 + f, TENSOR)
        k = half * TENSOR + to
        m = 2 * t + half
        is_own = (to == t) & (m == f)
        return (wire.at[k], out.at[f], send_a.at[k], recv_a.at[f], (m, to), is_own)

    @pl.loop(0, FSDP)
    def _(n):
        send(*stage_a(n))

    @pl.loop(0, FSDP)
    def _(n):
        arrived(out.at[n], recv_a.at[n])

    small_done(f, t, small, sums, sems)

    @pl.loop(0, FSDP)
    def _(n):
        sent(*stage_a(n))


def spread_kernel(
    wire, small, train, average, gains, send_a, recv_a, send_c, recv_c, rs, rr, cs, cr
):
    f = lax.axis_index("fsdp")
    t = lax.axis_index("tensor")
    sems = (rs, rr, cs, cr)
    enter(f, t, lambda i: (2 * t + i // TENSOR, lax.rem(i, TENSOR)))
    small_first(f, t, small, gains, sems)

    def stage_a(n):
        j = lax.rem(f + n + 2 * t, FSDP)
        k = lax.rem(f, 2) * TENSOR + t
        is_own = (j == f) & (f // 2 == t)
        return (wire.at[j], train.at[k], send_a.at[j], recv_a.at[k], (j, f // 2), is_own)

    def stage_c(n):
        k = lax.rem(n, 2) * TENSOR + lax.rem(n // 2 + f + t, TENSOR)
        return k, (train.at[k], average.at[f], send_c.at[k], recv_c.at[f], (k, t), k == f)

    @pl.loop(0, FSDP)
    def _(n):
        send(*stage_a(n))

    small_second(f, t, small, gains, sems)

    @pl.loop(0, FSDP)
    def _(n):
        k, copy = stage_c(n)
        arrived(train.at[k], recv_a.at[k])
        send(*copy)

    @pl.loop(0, FSDP)
    def _(n):
        arrived(average.at[n], recv_c.at[n])

    small_done(f, t, small, gains, sems)

    @pl.loop(0, FSDP)
    def _(n):
        sent(*stage_a(n))
        sent(*stage_c(n)[1])


def exchange(kernel, wire, small, outputs, relays, stages, collective_id):
    vmem = pl.BlockSpec(memory_space=pltpu.VMEM)
    pieces = jax.ShapeDtypeStruct(wire.shape, wire.dtype)
    dma = pltpu.SemaphoreType.DMA
    return pl.pallas_call(
        kernel,
        out_shape=[pieces] * outputs
        + [jax.ShapeDtypeStruct((FSDP, TENSOR) + small.shape, small.dtype)],
        in_specs=[vmem] * 2,
        out_specs=[vmem] * (outputs + 1),
        scratch_shapes=[pltpu.VMEM(wire.shape, wire.dtype)] * relays
        + [dma((FSDP,))] * (2 * stages)
        + [dma((TENSOR,)), dma((TENSOR,)), dma((FSDP,)), dma((FSDP,))],
        compiler_params=pltpu.CompilerParams(
            collective_id=collective_id, has_side_effects=True
        ),
    )(wire, small)


def total(x):
    wide = x.astype(jnp.float32)
    return jnp.sum(jnp.sum(wide * wide, axis=0, keepdims=True), axis=1, keepdims=True)


def same(shape, shift):
    i = lax.broadcasted_iota(jnp.int32, shape, 0)
    j = lax.broadcasted_iota(jnp.int32, shape, 1)
    return jnp.where(j == i + shift, 1.0, 0.0).astype(jnp.bfloat16)


def turn(a, b):
    return lax.dot_general(
        a, b, (((1,), (1,)), ((), ())), preferred_element_type=jnp.float32
    )


def put_tails(wire, k, tails):
    count, cols = tails.shape
    full = jnp.concatenate([tails, jnp.zeros((count, LANES - cols), jnp.float32)], axis=1)
    wire[k, pl.ds(wire.shape[1] - count, count), :] = full.astype(wire.dtype)


def unpack(pieces, k, layer, cols, unit):
    rest = pieces.shape[1] // 2 - cols
    head = turn(unit, pieces[k, pl.ds(layer * cols, cols), :])
    tails = pieces[k, pl.ds(2 * cols, 2 * rest), :].astype(jnp.float32)
    return jnp.concatenate([head, tails[layer * rest : (layer + 1) * rest, :cols]], axis=0)


def prepare_kernel(blocks, gains, wire, small):
    layers, cols, block_rows = blocks.shape
    rows = block_rows // FSDP
    rest = rows - LANES
    for k in range(FSDP):
        start = rows * k // LANES * LANES
        size = min(2 * LANES, block_rows - start)
        shift = rows * k - start
        chosen = same((LANES, size), shift)
        tails = jnp.zeros((layers * rest, cols), jnp.float32)
        for layer in range(layers):
            window = blocks[layer, :, pl.ds(start, size)]
            wire[k, pl.ds(layer * cols, cols), :] = turn(window, chosen).astype(wire.dtype)
            i = lax.broadcasted_iota(jnp.int32, (layers * rest, size), 0) - layer * rest
            j = lax.broadcasted_iota(jnp.int32, (layers * rest, size), 1) - shift - LANES
            hit = (i == j) & (i >= 0) & (i < rest)
            tails += turn(jnp.where(hit, 1.0, 0.0).astype(window.dtype), window)
        put_tails(wire, k, tails)
    squares = total(gains[...])
    for layer in range(layers):
        squares += total(blocks[layer])
    lane = lax.broadcasted_iota(jnp.int32, small.shape, 1)
    small[...] = jnp.where(lane == 0, squares, 0.0)


def joined(pieces, group, layer, unit):
    return jnp.concatenate(
        [unpack(pieces, 4 * group + i, layer, SPAN // 4, unit) for i in range(4)], axis=1
    )


def part(ref, buf, sem, layer, group, out):
    span = pl.ds(group * SPAN, SPAN)
    there, here = ref.at[:, layer, span], buf.at[layer, :, span]
    if out:
        there, here = here, there
    return pltpu.make_async_copy(there, here, sem.at[layer, group])


STEPS = [(layer, group) for group in range(4) for layer in range(2)]


def update_kernel(
    entries, pieces, sums, gain_grads, gain_master, gain_first, gain_second, gain_average,
    master, first, second,
    out_wire, gain_master_out, gain_first_out, gain_second_out, gain_average_out,
    master_out, first_out, second_out,
    master_buf, first_buf, second_buf, *sems,
):
    cols = SPAN // 4
    unit = same((LANES, LANES), 0)
    unit_cols = same((cols, cols), 0)
    tails = {}
    refs = (master, first, second)
    outs = (master_out, first_out, second_out)
    bufs = (master_buf, first_buf, second_buf)
    for step in STEPS:
        for i in range(3):
            part(refs[i], bufs[i], sems[i], *step, False).start()
    squares = jnp.sum(jnp.sum(sums[...], axis=0, keepdims=True), axis=1, keepdims=True)
    clip_scale = jnp.minimum(1.0, clip_level / jnp.sqrt(squares / entries + mean_epsilon))
    gain_news = adam_step(
        gain_grads[...], gain_master[...], gain_first[...], gain_second[...], clip_scale
    )
    gain_master_out[...], gain_first_out[...], gain_second_out[...] = gain_news
    gain_average_out[...] = (
        average_decay * gain_average[...] + (1.0 - average_decay) * gain_news[0]
    )
    for layer, group in STEPS:
        span = slice(group * SPAN, (group + 1) * SPAN)
        grads = joined(pieces, group, layer, unit)
        for i in range(3):
            part(refs[i], bufs[i], sems[i], layer, group, False).wait()
        news = adam_step(grads, *[buf[layer, :, span] for buf in bufs], clip_scale)
        for i in range(3):
            bufs[i][layer, :, span] = news[i]
            part(outs[i], bufs[i], sems[3 + i], layer, group, True).start()
        for i in range(4):
            piece = news[0][:, i * cols : (i + 1) * cols]
            out_wire[4 * group + i, pl.ds(layer * cols, cols), :] = turn(
                unit_cols, piece[:LANES].astype(out_wire.dtype)
            ).astype(out_wire.dtype)
            tails[i, layer] = piece[LANES:]
        if layer == 1:
            for i in range(4):
                both = jnp.concatenate([tails[i, 0], tails[i, 1]], axis=0)
                put_tails(out_wire, 4 * group + i, both)
    for step in STEPS:
        for i in range(3):
            part(outs[i], bufs[i], sems[3 + i], *step, True).wait()


def finish_kernel(
    train, pieces, average, train_out, average_out, buf, sem, sem_out, stack
):
    for step in STEPS:
        part(average, buf, sem, *step, False).start()
    unit = same((LANES, LANES), 0)
    for layer, group in STEPS:
        span = slice(group * SPAN, (group + 1) * SPAN)
        news = joined(pieces, group, layer, unit)
        part(average, buf, sem, layer, group, False).wait()
        buf[layer, :, span] = (
            average_decay * buf[layer, :, span] + (1.0 - average_decay) * news
        )
        part(average_out, buf, sem_out, layer, group, True).start()
    layers, cols, block_rows = train_out.shape
    rows = block_rows // FSDP
    unit_cols = same((cols, cols), 0)
    for layer in range(layers):
        for k in range(FSDP):
            stack[pl.ds(rows * k, rows), :] = unpack(train, k, layer, cols, unit)
        for start in range(0, block_rows, 2 * LANES):
            size = min(2 * LANES, block_rows - start)
            here = pl.ds(start, size)
            train_out[layer, :, here] = turn(
                unit_cols, stack[here, :].astype(jnp.bfloat16)
            ).astype(train_out.dtype)
    for step in STEPS:
        part(average_out, buf, sem_out, *step, True).wait()


def turned(x):
    return x.transpose(1, 0, 2)


def plain(kernel, outputs, out_specs, operands, specs, states, scratch=()):
    shape = (2, outputs[-1].shape[0], 4 * SPAN)
    return pl.pallas_call(
        kernel,
        out_shape=outputs,
        in_specs=specs,
        out_specs=out_specs,
        scratch_shapes=[pltpu.VMEM(shape, jnp.float32)] * states
        + [pltpu.SemaphoreType.DMA((2, 4))] * (2 * states)
        + list(scratch),
    )(*operands)


def on_device(
    grad_blocks,
    master_shard,
    first_moment,
    second_moment,
    average_shard,
    gain_grads,
    gain_master,
    gain_first,
    gain_second,
    gain_average,
):
    layers, block_rows, block_cols = grad_blocks.shape
    rows = block_rows // FSDP
    width = block_cols * FSDP
    entries = (grad_blocks.size + gain_grads.size) * FSDP * TENSOR

    vmem = pl.BlockSpec(memory_space=pltpu.VMEM)
    far = pl.BlockSpec(memory_space=pl.ANY)
    one_row = jax.ShapeDtypeStruct((1, LANES), jnp.float32)
    dense = layers * (block_cols + rows - LANES)
    wire_shape = jax.ShapeDtypeStruct((FSDP, dense, LANES), grad_blocks.dtype)
    flat = jax.ShapeDtypeStruct((rows, layers, width), jnp.float32)
    gain = jax.ShapeDtypeStruct(gain_master.shape, jnp.float32)

    wire, small = pl.pallas_call(
        prepare_kernel,
        out_shape=[wire_shape, one_row],
        in_specs=[vmem] * 2,
        out_specs=[vmem] * 2,
    )(grad_blocks.transpose(0, 2, 1), gain_grads)
    pieces, sums = exchange(gather_kernel, wire, small, 1, 0, 1, 0)

    (
        out_wire,
        master_gains,
        first_gains,
        second_gains,
        average_gains,
        master_next,
        first_next,
        second_next,
    ) = plain(
        functools.partial(update_kernel, entries),
        [wire_shape] + [gain] * 4 + [flat] * 3,
        [vmem] * 5 + [far] * 3,
        (
            pieces,
            sums.reshape(FSDP * TENSOR, LANES),
            gain_grads,
            gain_master,
            gain_first,
            gain_second,
            gain_average,
            turned(master_shard),
            turned(first_moment),
            turned(second_moment),
        ),
        [vmem] * 7 + [far] * 3,
        3,
    )
    train, averages, gains = exchange(spread_kernel, out_wire, master_gains, 2, 0, 2, 1)
    train_turned, average_next = plain(
        finish_kernel,
        [jax.ShapeDtypeStruct((layers, block_cols, block_rows), jnp.bfloat16), flat],
        [vmem, far],
        (train, averages, turned(average_shard)),
        [vmem, vmem, far],
        1,
        [pltpu.VMEM((block_rows, block_cols), jnp.float32)],
    )
    train_weights = train_turned.transpose(0, 2, 1)
    gain_weights = (
        gains.astype(jnp.bfloat16).transpose(2, 0, 1, 3).reshape(layers, -1)
    )
    return (
        train_weights,
        turned(master_next),
        turned(first_next),
        turned(second_next),
        turned(average_next),
        gain_weights,
        master_gains,
        first_gains,
        second_gains,
        average_gains,
    )


def solution(mesh):
    flat = P(None, ("fsdp", "tensor"), None)
    gain = P(None, ("fsdp", "tensor"))
    blocks = P(None, "tensor", "fsdp")
    averaging = P(None, ("tensor", "fsdp"), None)
    return jax.shard_map(
        on_device,
        mesh=mesh,
        in_specs=(blocks, flat, flat, flat, averaging, gain, gain, gain, gain, gain),
        out_specs=(blocks, flat, flat, flat, averaging, P(), gain, gain, gain, gain),
        check_vma=False,
    )
```

```python
import functools

import jax
import jax.numpy as jnp
from jax import lax
from jax.experimental import pallas as pl
from jax.experimental.pallas import tpu as pltpu
from jax.sharding import PartitionSpec as P

STEP = 20


learn_rate = 0.1
weight_decay = 0.1
beta_first = 0.9
beta_second = 0.95
adam_epsilon = 1e-08
average_decay = 0.9
clip_level = 0.5
mean_epsilon = 1e-06

MESH = pl.DeviceIdType.MESH
FSDP = 16
TENSOR = 8
LANES = 128
SPAN = 384


def adam_step(gradient, master, first_state, second_state, clip_scale):
    clipped = gradient.astype(jnp.float32) * clip_scale
    first_new = beta_first * first_state + (1.0 - beta_first) * clipped
    second_new = beta_second * second_state + (1.0 - beta_second) * clipped * clipped
    first_fix = 1.0 - beta_first**STEP
    second_fix = 1.0 - beta_second**STEP
    direction = (
        first_new / first_fix / (jnp.sqrt(second_new / second_fix) + adam_epsilon)
        + weight_decay * master
    )
    master_new = master - learn_rate * direction
    return (master_new, first_new, second_new)


def enter(f, t, sources=None):
    barrier = pltpu.get_barrier_semaphore()

    @pl.loop(1, TENSOR)
    def _(i):
        pl.semaphore_signal(
            barrier, inc=1, device_id=(f, lax.rem(t + i, TENSOR)), device_id_type=MESH
        )

    @pl.loop(1, FSDP)
    def _(i):
        pl.semaphore_signal(
            barrier, inc=1, device_id=(lax.rem(f + i, FSDP), t), device_id_type=MESH
        )

    peers = TENSOR + FSDP - 2
    if sources is not None:
        peers += FSDP - (f // 2 == t).astype(jnp.int32)

        @pl.loop(0, FSDP)
        def _(i):
            source_f, source_t = sources(i)

            @pl.when(jnp.logical_not((source_f == f) & (source_t == t)))
            def _():
                pl.semaphore_signal(
                    barrier, inc=1, device_id=(source_f, source_t), device_id_type=MESH
                )

    pl.semaphore_wait(barrier, peers)


def remote(source, target, send_sem, recv_sem, device):
    return pltpu.make_async_remote_copy(
        src_ref=source,
        dst_ref=target,
        send_sem=send_sem,
        recv_sem=recv_sem,
        device_id=device,
        device_id_type=MESH,
    )


def send(source, target, send_sem, recv_sem, device, is_own):
    @pl.when(is_own)
    def _():
        pltpu.make_async_copy(source, target, recv_sem).start()

    @pl.when(jnp.logical_not(is_own))
    def _():
        remote(source, target, send_sem, recv_sem, device).start()


def sent(source, target, send_sem, recv_sem, device, is_own):
    @pl.when(jnp.logical_not(is_own))
    def _():
        remote(source, target, send_sem, recv_sem, device).wait_send()


def arrived(target, recv_sem):
    pltpu.make_async_copy(target, target, recv_sem).wait()


def small_copies(f, t, small_ref, all_ref, sems):
    row_send, row_recv, col_send, col_recv = sems

    def row_copy(i):
        return remote(
            small_ref,
            all_ref.at[f, t],
            row_send.at[i],
            row_recv.at[t],
            (f, lax.rem(t + i, TENSOR)),
        )

    def col_copy(i):
        return remote(
            all_ref.at[f],
            all_ref.at[f],
            col_send.at[i],
            col_recv.at[f],
            (lax.rem(f + i, FSDP), t),
        )

    return row_copy, col_copy


def small_first(f, t, small_ref, all_ref, sems):
    row_copy, _ = small_copies(f, t, small_ref, all_ref, sems)
    pltpu.make_async_copy(small_ref, all_ref.at[f, t], sems[1].at[t]).start()

    @pl.loop(1, TENSOR)
    def _(i):
        row_copy(i).start()


def small_second(f, t, small_ref, all_ref, sems):
    _, col_copy = small_copies(f, t, small_ref, all_ref, sems)

    @pl.loop(0, TENSOR)
    def _(i):
        arrived(all_ref.at[f, i], sems[1].at[i])

    @pl.loop(1, FSDP)
    def _(i):
        col_copy(i).start()


def small_done(f, t, small_ref, all_ref, sems):
    row_copy, col_copy = small_copies(f, t, small_ref, all_ref, sems)

    @pl.loop(1, FSDP)
    def _(i):
        source = lax.rem(f + i, FSDP)
        arrived(all_ref.at[source], sems[3].at[source])

    @pl.loop(1, TENSOR)
    def _(i):
        row_copy(i).wait_send()

    @pl.loop(1, FSDP)
    def _(i):
        col_copy(i).wait_send()


def gather_kernel(wire, small, out, sums, send_a, recv_a, rs, rr, cs, cr):
    f = lax.axis_index("fsdp")
    t = lax.axis_index("tensor")
    sems = (rs, rr, cs, cr)
    enter(f, t, lambda i: (i, f // 2))
    small_first(f, t, small, sums, sems)

    def stage_a(n):
        half = lax.rem(n + f // TENSOR, 2)
        to = lax.rem(t + n // 2 + f, TENSOR)
        k = half * TENSOR + to
        m = 2 * t + half
        is_own = (to == t) & (m == f)
        return (wire.at[k], out.at[f], send_a.at[k], recv_a.at[f], (m, to), is_own)

    @pl.loop(0, 6)
    def _(n):
        send(*stage_a(n))

    small_second(f, t, small, sums, sems)

    @pl.loop(6, FSDP)
    def _(n):
        send(*stage_a(n))

    @pl.loop(0, FSDP)
    def _(n):
        arrived(out.at[n], recv_a.at[n])

    small_done(f, t, small, sums, sems)

    @pl.loop(0, FSDP)
    def _(n):
        sent(*stage_a(n))


def spread_kernel(
    wire, small, train, average, gains, mid,
    send_a, recv_a, send_b, recv_b, send_c, recv_c, rs, rr, cs, cr,
):
    f = lax.axis_index("fsdp")
    t = lax.axis_index("tensor")
    sems = (rs, rr, cs, cr)
    enter(f, t)
    small_first(f, t, small, gains, sems)

    def stage_a(n):
        j = lax.rem(f + n + 2 * t, FSDP)
        return (wire.at[j], mid.at[f], send_a.at[j], recv_a.at[f], (j, t), j == f)

    def stage_b(n):
        source = lax.rem(f - n - 2 * t + 2 * FSDP, FSDP)
        to = source // 2
        k = lax.rem(source, 2) * TENSOR + t
        return source, (
            mid.at[source], train.at[k], send_b.at[source], recv_b.at[k], (f, to), to == t,
        )

    def stage_c(n):
        turn_at = lax.rem(f - n + FSDP, FSDP)
        k = lax.rem(turn_at, 2) * TENSOR + lax.rem(turn_at // 2 - t + TENSOR, TENSOR)
        return k, (train.at[k], average.at[f], send_c.at[k], recv_c.at[f], (k, t), k == f)

    @pl.loop(0, FSDP)
    def _(n):
        send(*stage_a(n))

    @pl.loop(0, FSDP)
    def _(n):
        source, copy = stage_b(n)
        arrived(mid.at[source], recv_a.at[source])
        send(*copy)

    small_second(f, t, small, gains, sems)

    @pl.loop(0, FSDP)
    def _(n):
        k, copy = stage_c(n)
        arrived(train.at[k], recv_b.at[k])
        send(*copy)

    @pl.loop(0, FSDP)
    def _(n):
        arrived(average.at[n], recv_c.at[n])

    small_done(f, t, small, gains, sems)

    @pl.loop(0, FSDP)
    def _(n):
        sent(*stage_a(n))
        sent(*stage_b(n)[1])
        sent(*stage_c(n)[1])


def exchange(kernel, wire, small, outputs, relays, stages, collective_id):
    vmem = pl.BlockSpec(memory_space=pltpu.VMEM)
    pieces = jax.ShapeDtypeStruct(wire.shape, wire.dtype)
    dma = pltpu.SemaphoreType.DMA
    return pl.pallas_call(
        kernel,
        out_shape=[pieces] * outputs
        + [jax.ShapeDtypeStruct((FSDP, TENSOR) + small.shape, small.dtype)],
        in_specs=[vmem] * 2,
        out_specs=[vmem] * (outputs + 1),
        scratch_shapes=[pltpu.VMEM(wire.shape, wire.dtype)] * relays
        + [dma((FSDP,))] * (2 * stages)
        + [dma((TENSOR,)), dma((TENSOR,)), dma((FSDP,)), dma((FSDP,))],
        compiler_params=pltpu.CompilerParams(
            collective_id=collective_id, has_side_effects=True
        ),
    )(wire, small)


def total(x):
    wide = x.astype(jnp.float32)
    return jnp.sum(jnp.sum(wide * wide, axis=0, keepdims=True), axis=1, keepdims=True)


def same(shape, shift):
    i = lax.broadcasted_iota(jnp.int32, shape, 0)
    j = lax.broadcasted_iota(jnp.int32, shape, 1)
    return jnp.where(j == i + shift, 1.0, 0.0).astype(jnp.bfloat16)


def turn(a, b):
    return lax.dot_general(
        a, b, (((1,), (1,)), ((), ())), preferred_element_type=jnp.float32
    )


def put_tails(wire, k, tails):
    count, cols = tails.shape
    full = jnp.concatenate([tails, jnp.zeros((count, LANES - cols), jnp.float32)], axis=1)
    wire[k, pl.ds(wire.shape[1] - count, count), :] = full.astype(wire.dtype)


def unpack(pieces, k, layer, cols, unit):
    rest = pieces.shape[1] // 2 - cols
    head = turn(unit, pieces[k, pl.ds(layer * cols, cols), :])
    tails = pieces[k, pl.ds(2 * cols, 2 * rest), :].astype(jnp.float32)
    return jnp.concatenate([head, tails[layer * rest : (layer + 1) * rest, :cols]], axis=0)


def prepare_kernel(blocks, gains, wire, small):
    layers, cols, block_rows = blocks.shape
    rows = block_rows // FSDP
    rest = rows - LANES
    for k in range(FSDP):
        start = rows * k // LANES * LANES
        size = min(2 * LANES, block_rows - start)
        shift = rows * k - start
        chosen = same((LANES, size), shift)
        tails = jnp.zeros((layers * rest, cols), jnp.float32)
        for layer in range(layers):
            window = blocks[layer, :, pl.ds(start, size)]
            wire[k, pl.ds(layer * cols, cols), :] = turn(window, chosen).astype(wire.dtype)
            i = lax.broadcasted_iota(jnp.int32, (layers * rest, size), 0) - layer * rest
            j = lax.broadcasted_iota(jnp.int32, (layers * rest, size), 1) - shift - LANES
            hit = (i == j) & (i >= 0) & (i < rest)
            tails += turn(jnp.where(hit, 1.0, 0.0).astype(window.dtype), window)
        put_tails(wire, k, tails)
    squares = total(gains[...])
    for layer in range(layers):
        squares += total(blocks[layer])
    lane = lax.broadcasted_iota(jnp.int32, small.shape, 1)
    small[...] = jnp.where(lane == 0, squares, 0.0)


def joined(pieces, group, layer, unit):
    return jnp.concatenate(
        [unpack(pieces, 4 * group + i, layer, SPAN // 4, unit) for i in range(4)], axis=1
    )


def part(ref, buf, sem, layer, group, out):
    span = pl.ds(group * SPAN, SPAN)
    there, here = ref.at[:, layer, span], buf.at[layer, :, span]
    if out:
        there, here = here, there
    return pltpu.make_async_copy(there, here, sem.at[layer, group])


STEPS = [(layer, group) for group in range(4) for layer in range(2)]


def update_kernel(
    entries, pieces, sums, gain_grads, gain_master, gain_first, gain_second, gain_average,
    master, first, second,
    out_wire, gain_master_out, gain_first_out, gain_second_out, gain_average_out,
    master_out, first_out, second_out,
    master_buf, first_buf, second_buf, *sems,
):
    cols = SPAN // 4
    unit = same((LANES, LANES), 0)
    unit_cols = same((cols, cols), 0)
    tails = {}
    refs = (master, first, second)
    outs = (master_out, first_out, second_out)
    bufs = (master_buf, first_buf, second_buf)
    for step in STEPS:
        for i in range(3):
            part(refs[i], bufs[i], sems[i], *step, False).start()
    squares = jnp.sum(jnp.sum(sums[...], axis=0, keepdims=True), axis=1, keepdims=True)
    clip_scale = jnp.minimum(1.0, clip_level / jnp.sqrt(squares / entries + mean_epsilon))
    gain_news = adam_step(
        gain_grads[...], gain_master[...], gain_first[...], gain_second[...], clip_scale
    )
    gain_master_out[...], gain_first_out[...], gain_second_out[...] = gain_news
    gain_average_out[...] = (
        average_decay * gain_average[...] + (1.0 - average_decay) * gain_news[0]
    )
    for layer, group in STEPS:
        span = slice(group * SPAN, (group + 1) * SPAN)
        grads = joined(pieces, group, layer, unit)
        for i in range(3):
            part(refs[i], bufs[i], sems[i], layer, group, False).wait()
        news = adam_step(grads, *[buf[layer, :, span] for buf in bufs], clip_scale)
        for i in range(3):
            bufs[i][layer, :, span] = news[i]
            part(outs[i], bufs[i], sems[3 + i], layer, group, True).start()
        for i in range(4):
            piece = news[0][:, i * cols : (i + 1) * cols]
            out_wire[4 * group + i, pl.ds(layer * cols, cols), :] = turn(
                unit_cols, piece[:LANES].astype(out_wire.dtype)
            ).astype(out_wire.dtype)
            tails[i, layer] = piece[LANES:]
        if layer == 1:
            for i in range(4):
                both = jnp.concatenate([tails[i, 0], tails[i, 1]], axis=0)
                put_tails(out_wire, 4 * group + i, both)
    for step in STEPS:
        for i in range(3):
            part(outs[i], bufs[i], sems[3 + i], *step, True).wait()


def finish_kernel(
    train, pieces, average, train_out, average_out, buf, sem, sem_out, stack
):
    for step in STEPS:
        part(average, buf, sem, *step, False).start()
    unit = same((LANES, LANES), 0)
    for layer, group in STEPS:
        span = slice(group * SPAN, (group + 1) * SPAN)
        news = joined(pieces, group, layer, unit)
        part(average, buf, sem, layer, group, False).wait()
        buf[layer, :, span] = (
            average_decay * buf[layer, :, span] + (1.0 - average_decay) * news
        )
        part(average_out, buf, sem_out, layer, group, True).start()
    layers, cols, block_rows = train_out.shape
    rows = block_rows // FSDP
    unit_cols = same((cols, cols), 0)
    for layer in range(layers):
        for k in range(FSDP):
            stack[pl.ds(rows * k, rows), :] = unpack(train, k, layer, cols, unit)
        for start in range(0, block_rows, 2 * LANES):
            size = min(2 * LANES, block_rows - start)
            here = pl.ds(start, size)
            train_out[layer, :, here] = turn(
                unit_cols, stack[here, :].astype(jnp.bfloat16)
            ).astype(train_out.dtype)
    for step in STEPS:
        part(average_out, buf, sem_out, *step, True).wait()


def turned(x):
    return x.transpose(1, 0, 2)


def plain(kernel, outputs, out_specs, operands, specs, states, scratch=()):
    shape = (2, outputs[-1].shape[0], 4 * SPAN)
    return pl.pallas_call(
        kernel,
        out_shape=outputs,
        in_specs=specs,
        out_specs=out_specs,
        scratch_shapes=[pltpu.VMEM(shape, jnp.float32)] * states
        + [pltpu.SemaphoreType.DMA((2, 4))] * (2 * states)
        + list(scratch),
    )(*operands)


def on_device(
    grad_blocks,
    master_shard,
    first_moment,
    second_moment,
    average_shard,
    gain_grads,
    gain_master,
    gain_first,
    gain_second,
    gain_average,
):
    layers, block_rows, block_cols = grad_blocks.shape
    rows = block_rows // FSDP
    width = block_cols * FSDP
    entries = (grad_blocks.size + gain_grads.size) * FSDP * TENSOR

    vmem = pl.BlockSpec(memory_space=pltpu.VMEM)
    far = pl.BlockSpec(memory_space=pl.ANY)
    one_row = jax.ShapeDtypeStruct((1, LANES), jnp.float32)
    dense = layers * (block_cols + rows - LANES)
    wire_shape = jax.ShapeDtypeStruct((FSDP, dense, LANES), grad_blocks.dtype)
    flat = jax.ShapeDtypeStruct((rows, layers, width), jnp.float32)
    gain = jax.ShapeDtypeStruct(gain_master.shape, jnp.float32)

    wire, small = pl.pallas_call(
        prepare_kernel,
        out_shape=[wire_shape, one_row],
        in_specs=[vmem] * 2,
        out_specs=[vmem] * 2,
    )(grad_blocks.transpose(0, 2, 1), gain_grads)
    pieces, sums = exchange(gather_kernel, wire, small, 1, 0, 1, 0)

    (
        out_wire,
        master_gains,
        first_gains,
        second_gains,
        average_gains,
        master_next,
        first_next,
        second_next,
    ) = plain(
        functools.partial(update_kernel, entries),
        [wire_shape] + [gain] * 4 + [flat] * 3,
        [vmem] * 5 + [far] * 3,
        (
            pieces,
            sums.reshape(FSDP * TENSOR, LANES),
            gain_grads,
            gain_master,
            gain_first,
            gain_second,
            gain_average,
            turned(master_shard),
            turned(first_moment),
            turned(second_moment),
        ),
        [vmem] * 7 + [far] * 3,
        3,
    )
    train, averages, gains = exchange(spread_kernel, out_wire, master_gains, 2, 1, 3, 1)
    train_turned, average_next = plain(
        finish_kernel,
        [jax.ShapeDtypeStruct((layers, block_cols, block_rows), jnp.bfloat16), flat],
        [vmem, far],
        (train, averages, turned(average_shard)),
        [vmem, vmem, far],
        1,
        [pltpu.VMEM((block_rows, block_cols), jnp.float32)],
    )
    train_weights = train_turned.transpose(0, 2, 1)
    gain_weights = (
        gains.astype(jnp.bfloat16).transpose(2, 0, 1, 3).reshape(layers, -1)
    )
    return (
        train_weights,
        turned(master_next),
        turned(first_next),
        turned(second_next),
        turned(average_next),
        gain_weights,
        master_gains,
        first_gains,
        second_gains,
        average_gains,
    )


def solution(mesh):
    flat = P(None, ("fsdp", "tensor"), None)
    gain = P(None, ("fsdp", "tensor"))
    blocks = P(None, "tensor", "fsdp")
    averaging = P(None, ("tensor", "fsdp"), None)
    return jax.shard_map(
        on_device,
        mesh=mesh,
        in_specs=(blocks, flat, flat, flat, averaging, gain, gain, gain, gain, gain),
        out_specs=(blocks, flat, flat, flat, averaging, P(), gain, gain, gain, gain),
        check_vma=False,
    )
```

```python
import functools

import jax
import jax.numpy as jnp
from jax import lax
from jax.experimental import pallas as pl
from jax.experimental.pallas import tpu as pltpu
from jax.sharding import PartitionSpec as P

STEP = 20


learn_rate = 0.1
weight_decay = 0.1
beta_first = 0.9
beta_second = 0.95
adam_epsilon = 1e-08
average_decay = 0.9
clip_level = 0.5
mean_epsilon = 1e-06

MESH = pl.DeviceIdType.MESH
FSDP = 16
TENSOR = 8
LANES = 128
SPAN = 384
LAG = 4


def adam_step(gradient, master, first_state, second_state, clip_scale):
    clipped = gradient.astype(jnp.float32) * clip_scale
    first_new = beta_first * first_state + (1.0 - beta_first) * clipped
    second_new = beta_second * second_state + (1.0 - beta_second) * clipped * clipped
    first_fix = 1.0 - beta_first**STEP
    second_fix = 1.0 - beta_second**STEP
    direction = (
        first_new / first_fix / (jnp.sqrt(second_new / second_fix) + adam_epsilon)
        + weight_decay * master
    )
    master_new = master - learn_rate * direction
    return (master_new, first_new, second_new)


def enter(f, t, sources=None):
    barrier = pltpu.get_barrier_semaphore()

    @pl.loop(1, TENSOR)
    def _(i):
        pl.semaphore_signal(
            barrier, inc=1, device_id=(f, lax.rem(t + i, TENSOR)), device_id_type=MESH
        )

    @pl.loop(1, FSDP)
    def _(i):
        pl.semaphore_signal(
            barrier, inc=1, device_id=(lax.rem(f + i, FSDP), t), device_id_type=MESH
        )

    peers = TENSOR + FSDP - 2
    if sources is not None:
        peers += FSDP - (f // 2 == t).astype(jnp.int32)

        @pl.loop(0, FSDP)
        def _(i):
            source_f, source_t = sources(i)

            @pl.when(jnp.logical_not((source_f == f) & (source_t == t)))
            def _():
                pl.semaphore_signal(
                    barrier, inc=1, device_id=(source_f, source_t), device_id_type=MESH
                )

    pl.semaphore_wait(barrier, peers)


def remote(source, target, send_sem, recv_sem, device):
    return pltpu.make_async_remote_copy(
        src_ref=source,
        dst_ref=target,
        send_sem=send_sem,
        recv_sem=recv_sem,
        device_id=device,
        device_id_type=MESH,
    )


def send(source, target, send_sem, recv_sem, device, is_own):
    @pl.when(is_own)
    def _():
        pltpu.make_async_copy(source, target, recv_sem).start()

    @pl.when(jnp.logical_not(is_own))
    def _():
        remote(source, target, send_sem, recv_sem, device).start()


def sent(source, target, send_sem, recv_sem, device, is_own):
    @pl.when(jnp.logical_not(is_own))
    def _():
        remote(source, target, send_sem, recv_sem, device).wait_send()


def arrived(target, recv_sem):
    pltpu.make_async_copy(target, target, recv_sem).wait()


def small_copies(f, t, small_ref, all_ref, sems):
    row_send, row_recv, col_send, col_recv = sems

    def row_copy(i):
        return remote(
            small_ref,
            all_ref.at[f, t],
            row_send.at[i],
            row_recv.at[t],
            (f, lax.rem(t + i, TENSOR)),
        )

    def col_copy(i):
        return remote(
            all_ref.at[f],
            all_ref.at[f],
            col_send.at[i],
            col_recv.at[f],
            (lax.rem(f + i, FSDP), t),
        )

    return row_copy, col_copy


def small_first(f, t, small_ref, all_ref, sems):
    row_copy, _ = small_copies(f, t, small_ref, all_ref, sems)
    pltpu.make_async_copy(small_ref, all_ref.at[f, t], sems[1].at[t]).start()

    @pl.loop(1, TENSOR)
    def _(i):
        row_copy(i).start()


def small_second(f, t, small_ref, all_ref, sems):
    _, col_copy = small_copies(f, t, small_ref, all_ref, sems)

    @pl.loop(0, TENSOR)
    def _(i):
        arrived(all_ref.at[f, i], sems[1].at[i])

    @pl.loop(1, FSDP)
    def _(i):
        col_copy(i).start()


def small_done(f, t, small_ref, all_ref, sems):
    row_copy, col_copy = small_copies(f, t, small_ref, all_ref, sems)

    @pl.loop(1, FSDP)
    def _(i):
        source = lax.rem(f + i, FSDP)
        arrived(all_ref.at[source], sems[3].at[source])

    @pl.loop(1, TENSOR)
    def _(i):
        row_copy(i).wait_send()

    @pl.loop(1, FSDP)
    def _(i):
        col_copy(i).wait_send()


def gather_kernel(wire, small, out, sums, send_a, recv_a, rs, rr, cs, cr):
    f = lax.axis_index("fsdp")
    t = lax.axis_index("tensor")
    sems = (rs, rr, cs, cr)
    enter(f, t, lambda i: (i, f // 2))
    small_first(f, t, small, sums, sems)

    def stage_a(n):
        half = lax.rem(n + f // TENSOR, 2)
        to = lax.rem(t + n // 2 + f, TENSOR)
        k = half * TENSOR + to
        m = 2 * t + half
        is_own = (to == t) & (m == f)
        return (wire.at[k], out.at[f], send_a.at[k], recv_a.at[f], (m, to), is_own)

    @pl.loop(0, 6)
    def _(n):
        send(*stage_a(n))

    small_second(f, t, small, sums, sems)

    @pl.loop(6, FSDP)
    def _(n):
        send(*stage_a(n))

    @pl.loop(0, FSDP)
    def _(n):
        arrived(out.at[n], recv_a.at[n])

    small_done(f, t, small, sums, sems)

    @pl.loop(0, FSDP)
    def _(n):
        sent(*stage_a(n))


def spread_kernel(
    wire, small, train, average, gains, mid,
    send_a, recv_a, send_b, recv_b, send_c, recv_c, rs, rr, cs, cr,
):
    f = lax.axis_index("fsdp")
    t = lax.axis_index("tensor")
    sems = (rs, rr, cs, cr)
    enter(f, t)
    small_first(f, t, small, gains, sems)

    def stage_a(n):
        j = lax.rem(f + n + 2 * t, FSDP)
        return (wire.at[j], mid.at[f], send_a.at[j], recv_a.at[f], (j, t), j == f)

    def stage_b(n):
        source = lax.rem(f - n - 2 * t + 2 * FSDP, FSDP)
        to = source // 2
        k = lax.rem(source, 2) * TENSOR + t
        return source, (
            mid.at[source], train.at[k], send_b.at[source], recv_b.at[k], (f, to), to == t,
        )

    def stage_c(n):
        turn_at = lax.rem(f - n + FSDP, FSDP)
        k = lax.rem(turn_at, 2) * TENSOR + lax.rem(turn_at // 2 - t + TENSOR, TENSOR)
        return k, (train.at[k], average.at[f], send_c.at[k], recv_c.at[f], (k, t), k == f)

    @pl.loop(0, FSDP)
    def _(n):
        send(*stage_a(n))

    small_second(f, t, small, gains, sems)

    @pl.loop(0, FSDP + LAG)
    def _(n):
        @pl.when(n < FSDP)
        def _():
            source, copy = stage_b(n)
            arrived(mid.at[source], recv_a.at[source])
            send(*copy)

        @pl.when(n >= LAG)
        def _():
            k, copy = stage_c(n - LAG)
            arrived(train.at[k], recv_b.at[k])
            send(*copy)

    @pl.loop(0, FSDP)
    def _(n):
        arrived(average.at[n], recv_c.at[n])

    small_done(f, t, small, gains, sems)

    @pl.loop(0, FSDP)
    def _(n):
        sent(*stage_a(n))
        sent(*stage_b(n)[1])
        sent(*stage_c(n)[1])


def exchange(kernel, wire, small, outputs, relays, stages, collective_id):
    vmem = pl.BlockSpec(memory_space=pltpu.VMEM)
    pieces = jax.ShapeDtypeStruct(wire.shape, wire.dtype)
    dma = pltpu.SemaphoreType.DMA
    return pl.pallas_call(
        kernel,
        out_shape=[pieces] * outputs
        + [jax.ShapeDtypeStruct((FSDP, TENSOR) + small.shape, small.dtype)],
        in_specs=[vmem] * 2,
        out_specs=[vmem] * (outputs + 1),
        scratch_shapes=[pltpu.VMEM(wire.shape, wire.dtype)] * relays
        + [dma((FSDP,))] * (2 * stages)
        + [dma((TENSOR,)), dma((TENSOR,)), dma((FSDP,)), dma((FSDP,))],
        compiler_params=pltpu.CompilerParams(
            collective_id=collective_id, has_side_effects=True
        ),
    )(wire, small)


def total(x):
    wide = x.astype(jnp.float32)
    return jnp.sum(jnp.sum(wide * wide, axis=0, keepdims=True), axis=1, keepdims=True)


def same(shape, shift):
    i = lax.broadcasted_iota(jnp.int32, shape, 0)
    j = lax.broadcasted_iota(jnp.int32, shape, 1)
    return jnp.where(j == i + shift, 1.0, 0.0).astype(jnp.bfloat16)


def turn(a, b):
    return lax.dot_general(
        a, b, (((1,), (1,)), ((), ())), preferred_element_type=jnp.float32
    )


def put_tails(wire, k, tails):
    count, cols = tails.shape
    full = jnp.concatenate([tails, jnp.zeros((count, LANES - cols), jnp.float32)], axis=1)
    wire[k, pl.ds(wire.shape[1] - count, count), :] = full.astype(wire.dtype)


def unpack(pieces, k, layer, cols, unit):
    rest = pieces.shape[1] // 2 - cols
    head = turn(unit, pieces[k, pl.ds(layer * cols, cols), :])
    tails = pieces[k, pl.ds(2 * cols, 2 * rest), :].astype(jnp.float32)
    return jnp.concatenate([head, tails[layer * rest : (layer + 1) * rest, :cols]], axis=0)


def prepare_kernel(blocks, gains, wire, small):
    layers, cols, block_rows = blocks.shape
    rows = block_rows // FSDP
    rest = rows - LANES
    for k in range(FSDP):
        start = rows * k // LANES * LANES
        size = min(2 * LANES, block_rows - start)
        shift = rows * k - start
        chosen = same((LANES, size), shift)
        tails = jnp.zeros((layers * rest, cols), jnp.float32)
        for layer in range(layers):
            window = blocks[layer, :, pl.ds(start, size)]
            wire[k, pl.ds(layer * cols, cols), :] = turn(window, chosen).astype(wire.dtype)
            i = lax.broadcasted_iota(jnp.int32, (layers * rest, size), 0) - layer * rest
            j = lax.broadcasted_iota(jnp.int32, (layers * rest, size), 1) - shift - LANES
            hit = (i == j) & (i >= 0) & (i < rest)
            tails += turn(jnp.where(hit, 1.0, 0.0).astype(window.dtype), window)
        put_tails(wire, k, tails)
    squares = total(gains[...])
    for layer in range(layers):
        squares += total(blocks[layer])
    lane = lax.broadcasted_iota(jnp.int32, small.shape, 1)
    small[...] = jnp.where(lane == 0, squares, 0.0)


def joined(pieces, group, layer, unit):
    return jnp.concatenate(
        [unpack(pieces, 4 * group + i, layer, SPAN // 4, unit) for i in range(4)], axis=1
    )


def part(ref, buf, sem, layer, group, out):
    span = pl.ds(group * SPAN, SPAN)
    there, here = ref.at[:, layer, span], buf.at[layer, :, span]
    if out:
        there, here = here, there
    return pltpu.make_async_copy(there, here, sem.at[layer, group])


STEPS = [(layer, group) for group in range(4) for layer in range(2)]


def update_kernel(
    entries, pieces, sums, gain_grads, gain_master, gain_first, gain_second, gain_average,
    master, first, second,
    out_wire, gain_master_out, gain_first_out, gain_second_out, gain_average_out,
    master_out, first_out, second_out,
    master_buf, first_buf, second_buf, *sems,
):
    cols = SPAN // 4
    unit = same((LANES, LANES), 0)
    unit_cols = same((cols, cols), 0)
    tails = {}
    refs = (master, first, second)
    outs = (master_out, first_out, second_out)
    bufs = (master_buf, first_buf, second_buf)
    for step in STEPS:
        for i in range(3):
            part(refs[i], bufs[i], sems[i], *step, False).start()
    squares = jnp.sum(jnp.sum(sums[...], axis=0, keepdims=True), axis=1, keepdims=True)
    clip_scale = jnp.minimum(1.0, clip_level / jnp.sqrt(squares / entries + mean_epsilon))
    gain_news = adam_step(
        gain_grads[...], gain_master[...], gain_first[...], gain_second[...], clip_scale
    )
    gain_master_out[...], gain_first_out[...], gain_second_out[...] = gain_news
    gain_average_out[...] = (
        average_decay * gain_average[...] + (1.0 - average_decay) * gain_news[0]
    )
    for layer, group in STEPS:
        span = slice(group * SPAN, (group + 1) * SPAN)
        grads = joined(pieces, group, layer, unit)
        for i in range(3):
            part(refs[i], bufs[i], sems[i], layer, group, False).wait()
        news = adam_step(grads, *[buf[layer, :, span] for buf in bufs], clip_scale)
        for i in range(3):
            bufs[i][layer, :, span] = news[i]
            part(outs[i], bufs[i], sems[3 + i], layer, group, True).start()
        for i in range(4):
            piece = news[0][:, i * cols : (i + 1) * cols]
            out_wire[4 * group + i, pl.ds(layer * cols, cols), :] = turn(
                unit_cols, piece[:LANES].astype(out_wire.dtype)
            ).astype(out_wire.dtype)
            tails[i, layer] = piece[LANES:]
        if layer == 1:
            for i in range(4):
                both = jnp.concatenate([tails[i, 0], tails[i, 1]], axis=0)
                put_tails(out_wire, 4 * group + i, both)
    for step in STEPS:
        for i in range(3):
            part(outs[i], bufs[i], sems[3 + i], *step, True).wait()


def finish_kernel(
    train, pieces, average, train_out, average_out, buf, sem, sem_out, stack
):
    for step in STEPS:
        part(average, buf, sem, *step, False).start()
    unit = same((LANES, LANES), 0)
    for layer, group in STEPS:
        span = slice(group * SPAN, (group + 1) * SPAN)
        news = joined(pieces, group, layer, unit)
        part(average, buf, sem, layer, group, False).wait()
        buf[layer, :, span] = (
            average_decay * buf[layer, :, span] + (1.0 - average_decay) * news
        )
        part(average_out, buf, sem_out, layer, group, True).start()
    layers, cols, block_rows = train_out.shape
    rows = block_rows // FSDP
    unit_cols = same((cols, cols), 0)
    for layer in range(layers):
        for k in range(FSDP):
            stack[pl.ds(rows * k, rows), :] = unpack(train, k, layer, cols, unit)
        for start in range(0, block_rows, 2 * LANES):
            size = min(2 * LANES, block_rows - start)
            here = pl.ds(start, size)
            train_out[layer, :, here] = turn(
                unit_cols, stack[here, :].astype(jnp.bfloat16)
            ).astype(train_out.dtype)
    for step in STEPS:
        part(average_out, buf, sem_out, *step, True).wait()


def turned(x):
    return x.transpose(1, 0, 2)


def plain(kernel, outputs, out_specs, operands, specs, states, scratch=()):
    shape = (2, outputs[-1].shape[0], 4 * SPAN)
    return pl.pallas_call(
        kernel,
        out_shape=outputs,
        in_specs=specs,
        out_specs=out_specs,
        scratch_shapes=[pltpu.VMEM(shape, jnp.float32)] * states
        + [pltpu.SemaphoreType.DMA((2, 4))] * (2 * states)
        + list(scratch),
    )(*operands)


def on_device(
    grad_blocks,
    master_shard,
    first_moment,
    second_moment,
    average_shard,
    gain_grads,
    gain_master,
    gain_first,
    gain_second,
    gain_average,
):
    layers, block_rows, block_cols = grad_blocks.shape
    rows = block_rows // FSDP
    width = block_cols * FSDP
    entries = (grad_blocks.size + gain_grads.size) * FSDP * TENSOR

    vmem = pl.BlockSpec(memory_space=pltpu.VMEM)
    far = pl.BlockSpec(memory_space=pl.ANY)
    one_row = jax.ShapeDtypeStruct((1, LANES), jnp.float32)
    dense = layers * (block_cols + rows - LANES)
    wire_shape = jax.ShapeDtypeStruct((FSDP, dense, LANES), grad_blocks.dtype)
    flat = jax.ShapeDtypeStruct((rows, layers, width), jnp.float32)
    gain = jax.ShapeDtypeStruct(gain_master.shape, jnp.float32)

    wire, small = pl.pallas_call(
        prepare_kernel,
        out_shape=[wire_shape, one_row],
        in_specs=[vmem] * 2,
        out_specs=[vmem] * 2,
    )(grad_blocks.transpose(0, 2, 1), gain_grads)
    pieces, sums = exchange(gather_kernel, wire, small, 1, 0, 1, 0)

    (
        out_wire,
        master_gains,
        first_gains,
        second_gains,
        average_gains,
        master_next,
        first_next,
        second_next,
    ) = plain(
        functools.partial(update_kernel, entries),
        [wire_shape] + [gain] * 4 + [flat] * 3,
        [vmem] * 5 + [far] * 3,
        (
            pieces,
            sums.reshape(FSDP * TENSOR, LANES),
            gain_grads,
            gain_master,
            gain_first,
            gain_second,
            gain_average,
            turned(master_shard),
            turned(first_moment),
            turned(second_moment),
        ),
        [vmem] * 7 + [far] * 3,
        3,
    )
    train, averages, gains = exchange(spread_kernel, out_wire, master_gains, 2, 1, 3, 1)
    train_turned, average_next = plain(
        finish_kernel,
        [jax.ShapeDtypeStruct((layers, block_cols, block_rows), jnp.bfloat16), flat],
        [vmem, far],
        (train, averages, turned(average_shard)),
        [vmem, vmem, far],
        1,
        [pltpu.VMEM((block_rows, block_cols), jnp.float32)],
    )
    train_weights = train_turned.transpose(0, 2, 1)
    gain_weights = (
        gains.astype(jnp.bfloat16).transpose(2, 0, 1, 3).reshape(layers, -1)
    )
    return (
        train_weights,
        turned(master_next),
        turned(first_next),
        turned(second_next),
        turned(average_next),
        gain_weights,
        master_gains,
        first_gains,
        second_gains,
        average_gains,
    )


def solution(mesh):
    flat = P(None, ("fsdp", "tensor"), None)
    gain = P(None, ("fsdp", "tensor"))
    blocks = P(None, "tensor", "fsdp")
    averaging = P(None, ("tensor", "fsdp"), None)
    return jax.shard_map(
        on_device,
        mesh=mesh,
        in_specs=(blocks, flat, flat, flat, averaging, gain, gain, gain, gain, gain),
        out_specs=(blocks, flat, flat, flat, averaging, P(), gain, gain, gain, gain),
        check_vma=False,
    )
```
